512 devices in a mesh: rows: 64 (over y, z), grp: 8 (over x, core).
Axes of the slice: x: 4, y: 8, z: 8, core: 2. Of those that a mesh axis runs over, the one named last changes fastest.
Arguments:
- basis: float32 [64, 2097152], P(None, ('rows', 'grp'))
- values: float32 [64], replicated, may hold values from 0.5 to 20
- archive: bfloat16 [64, 2097152], P('grp', 'rows')
- window_ids: int32 [32], replicated, may hold values from 0 to 63, as said below
Outputs:
- filtered: float32 [96, 2097152], P(None, ('rows', 'grp'))
- projector: float32 [96, 96], replicated
- novelty: float32 [32], replicated
The draws below stay inside these ranges and needn't reach their ends.
Inputs may be any that keep to these rules, and one draw needn't show every extreme that they name: `window_ids`: distinct; 0 and 63 are always among them.
All inputs are finite; a program needn't handle non-finite values.
Results may differ from the reference program's by a relative error of at most 0.0003.
Values may be sent and summed in bfloat16 or wider, within the bound.
No kernel may reach another device: no remote copies, remote signals or barrier semaphores. Data moves between devices by JAX's collectives and lax.ppermute only.
A program may use at most 64 MiB of HBM per device.

```python
import math
import jax
import jax.numpy as jnp
from jax import lax

MODES = 64
WINDOWS = 32
ARCHIVE = 64
NEWTON = 10
SPACE_LAG = 2097152


pair_gap = 0.003


signal_gain = 0.7


common_gain = 0.5


mode_spread = 0.05


def shared_basis(key):
    entries = jax.random.normal(jax.random.fold_in(key, 11), (MODES, SPACE_LAG), jnp.float32)
    gains = jnp.exp(jax.random.uniform(jax.random.fold_in(key, 18), (MODES, 1), jnp.float32, -mode_spread, mode_spread))
    return entries * gains * (1.0 / math.sqrt(SPACE_LAG))


def draw_basis(key, part):
    return shared_basis(key)


def draw_archive(key, part):
    basis = shared_basis(key)
    chosen = jax.random.randint(jax.random.fold_in(key, 12), (ARCHIVE, 3), 0, MODES)
    coeffs = jax.random.normal(jax.random.fold_in(key, 13), (ARCHIVE, 3), jnp.float32) * signal_gain
    signal = coeffs[:, 0:1] * basis[chosen[:, 0]]
    signal = signal + coeffs[:, 1:2] * basis[chosen[:, 1]]
    signal = signal + coeffs[:, 2:3] * basis[chosen[:, 2]]
    signal = signal * math.sqrt(SPACE_LAG)
    position = jnp.arange(SPACE_LAG, dtype=jnp.float32) / SPACE_LAG
    noise = jax.random.normal(jax.random.fold_in(key, 14), (ARCHIVE, SPACE_LAG), jnp.float32)
    fresh = jax.random.normal(jax.random.fold_in(key, 17), (ARCHIVE, SPACE_LAG), jnp.float32)
    common = jax.random.normal(jax.random.fold_in(key, 20), (SPACE_LAG,), jnp.float32)
    rough = jnp.exp(jax.random.uniform(jax.random.fold_in(key, 15), (SPACE_LAG,), jnp.float32, 0.0, math.log(10.0)))
    heights = jax.random.normal(jax.random.fold_in(key, 23), (ARCHIVE, 1), jnp.float32) * common_gain
    base = signal + noise + heights * common[None, :]
    lower = (jnp.arange(ARCHIVE) < ARCHIVE // 2)[:, None]
    paired = jnp.where(lower, base, base[::-1] + pair_gap * (common[None, :] + fresh))
    row_scale = jnp.exp(math.log(3.0) * position) * rough
    col_scale = jnp.exp(jax.random.uniform(jax.random.fold_in(key, 16), (ARCHIVE, 1), jnp.float32, 0.0, math.log(10.0)))
    return (col_scale * row_scale[None, :] * paired).astype(jnp.bfloat16)


def draw_window_ids(key, part):
    inner = jax.random.permutation(jax.random.fold_in(key, 21), ARCHIVE - 2)[:WINDOWS - 2] + 1
    ends = jnp.array([0, ARCHIVE - 1], dtype=jnp.int32)
    joined = jnp.concatenate([ends, inner.astype(jnp.int32)])
    return jax.random.permutation(jax.random.fold_in(key, 22), joined).astype(jnp.int32)


def setup_inputs(seed: int = 0) -> dict:
    arg_keys = jax.random.split(jax.random.key(seed), 5)
    return {
        "basis": draw_basis(jax.random.fold_in(arg_keys[4], 71), 0),
        "values": jnp.clip(jnp.exp(jax.random.uniform(arg_keys[1], (MODES,), jnp.float32, math.log(0.5), math.log(20.0))), 0.5, 20.0),
        "archive": draw_archive(jax.random.fold_in(arg_keys[4], 71), 0),
        "window_ids": draw_window_ids(jax.random.fold_in(arg_keys[4], 71), 0),
    }


HIGH = lax.Precision.HIGHEST

def spectral(core):
    width = core.shape[0]
    identity = jnp.eye(width, dtype=jnp.float32)
    square = jnp.dot(core, core.T, precision=HIGH)
    total = jnp.trace(square)
    shifted = (square - total / width * identity) / total
    for iteration in range(NEWTON):
        cubed = jnp.dot(jnp.dot(shifted, shifted, precision=HIGH), shifted, precision=HIGH)
        shifted = 1.5 * shifted - 0.5 * cubed
    return 0.5 * (identity + shifted)

def inverse_lower(gram):
    factor = jnp.linalg.cholesky(gram)
    identity = jnp.eye(gram.shape[0], dtype=jnp.float32)
    return (factor, jax.scipy.linalg.solve_triangular(factor, identity, lower=True))

def reference(basis, values, archive, window_ids):
    columns = archive[window_ids].astype(jnp.float32) * (1.0 / math.sqrt(SPACE_LAG))
    projection = jnp.dot(basis, columns.T, precision=HIGH)
    energy = lax.optimization_barrier(jnp.sum(columns * columns, axis=1))
    resid = columns - jnp.dot(projection.T, basis, precision=HIGH)
    gram_one = jnp.dot(resid, resid.T, precision=HIGH)
    factor_one, inverse_one = inverse_lower(gram_one)
    first = jnp.dot(inverse_one, resid, precision=HIGH)
    gram_two = jnp.dot(first, first.T, precision=HIGH)
    factor_two, inverse_two = inverse_lower(gram_two)
    ortho = jnp.dot(inverse_two, first, precision=HIGH)
    upper = jnp.dot(factor_two.T, factor_one.T, precision=HIGH)
    top_rows = jnp.concatenate([jnp.diag(values), projection], axis=1)
    low_rows = jnp.concatenate([jnp.zeros((WINDOWS, MODES), jnp.float32), upper], axis=1)
    core = jnp.concatenate([top_rows, low_rows], axis=0)
    projector = spectral(core)
    weights = jnp.dot(core.T, projector, precision=HIGH)
    stacked = jnp.concatenate([basis, ortho], axis=0)
    filtered = jnp.dot(weights, stacked, precision=HIGH) * math.sqrt(SPACE_LAG)
    novelty = jnp.diagonal(gram_one) / energy
    return (filtered, projector, novelty)
```

```python
import math

import jax
import jax.numpy as jnp
from jax import lax
from jax.sharding import Mesh, PartitionSpec as P

NEWTON = 10
HIGH = lax.Precision.HIGHEST
ALL = ("y", "z", "x", "c")


def spectral(core):
    width = core.shape[0]
    identity = jnp.eye(width, dtype=jnp.float32)
    square = jnp.dot(core, core.T, precision=HIGH)
    total = jnp.trace(square)
    shifted = (square - total / width * identity) / total
    for iteration in range(NEWTON):
        cubed = jnp.dot(jnp.dot(shifted, shifted, precision=HIGH), shifted, precision=HIGH)
        shifted = 1.5 * shifted - 0.5 * cubed
    return 0.5 * (identity + shifted)


def inverse_lower(gram):
    factor = jnp.linalg.cholesky(gram)
    identity = jnp.eye(gram.shape[0], dtype=jnp.float32)
    return (factor, jax.scipy.linalg.solve_triangular(factor, identity, lower=True))


def sum_over(block, axes):
    count = 1
    for name in axes:
        count *= lax.axis_size(name)
    copies = jnp.broadcast_to(block[None], (count,) + block.shape)
    return jnp.sum(lax.all_to_all(copies, axes, 0, 0, tiled=True), axis=0)


def total_sum(block):
    return sum_over(sum_over(block, ("y", "x")), ("z", "c"))


def per_device(basis, values, archive, window_ids):
    mode_count = basis.shape[0]
    window_count = window_ids.shape[0]
    local_rows = basis.shape[1]
    total_rows = local_rows
    for name in ALL:
        total_rows *= lax.axis_size(name)
    everything = lax.all_to_all(archive, ("x", "c"), split_axis=1, concat_axis=0, tiled=True)
    picker = (
        window_ids[:, None] == jnp.arange(everything.shape[0], dtype=jnp.int32)[None, :]
    ).astype(jnp.bfloat16)
    gathered = jnp.dot(picker, everything, preferred_element_type=jnp.float32)
    columns = gathered * (1.0 / math.sqrt(total_rows))
    proj_part = jnp.einsum("kr,pr->kp", basis, columns, precision=HIGH)
    energy_part = jnp.sum(columns * columns, axis=1)
    packed = jnp.concatenate([proj_part, energy_part[None, :], jnp.zeros((7, window_count), jnp.float32)], axis=0)
    packed = total_sum(packed.reshape(-1, 128)).reshape(packed.shape)
    projection = packed[:mode_count]
    energy = packed[mode_count]
    resid = columns - jnp.einsum("kp,kr->pr", projection, basis, precision=HIGH)
    gram_one = jnp.einsum("pr,qr->pq", resid, resid, precision=HIGH)
    gram_one = total_sum(gram_one.reshape(-1, 128)).reshape(gram_one.shape)
    factor_one, inverse_one = inverse_lower(gram_one)
    first = jnp.dot(inverse_one, resid, precision=HIGH)
    gram_two = jnp.einsum("pr,qr->pq", first, first, precision=HIGH)
    gram_two = total_sum(gram_two.reshape(-1, 128)).reshape(gram_two.shape)
    factor_two, inverse_two = inverse_lower(gram_two)
    ortho = jnp.dot(inverse_two, first, precision=HIGH)
    upper = jnp.dot(factor_two.T, factor_one.T, precision=HIGH)
    top_rows = jnp.concatenate([jnp.diag(values), projection], axis=1)
    low_rows = jnp.concatenate([jnp.zeros((window_count, mode_count), jnp.float32), upper], axis=1)
    core = jnp.concatenate([top_rows, low_rows], axis=0)
    projector = spectral(core)
    weights = jnp.dot(core.T, projector, precision=HIGH)
    stacked = jnp.concatenate([basis, ortho], axis=0)
    filtered = jnp.dot(weights, stacked, precision=HIGH) * math.sqrt(total_rows)
    novelty = jnp.diagonal(gram_one) / energy
    return (filtered, projector, novelty)


def solution(mesh):
    fine = Mesh(mesh.devices.reshape(8, 8, 4, 2), ALL)
    placed = (P(None, ALL), P(), P(("x", "c"), ("y", "z")), P())
    return jax.shard_map(
        per_device,
        mesh=fine,
        in_specs=placed,
        out_specs=(P(None, ALL), P(), P()),
        check_vma=False,
    )
```

```python
import math

import jax
import jax.numpy as jnp
from jax import lax
from jax.experimental import pallas as pl
from jax.experimental.pallas import tpu as pltpu
from jax.sharding import Mesh, PartitionSpec as P

NEWTON = 10
HIGH = lax.Precision.HIGHEST
ALL = ("y", "z", "x", "c")
F32 = jnp.float32
BF16 = jnp.bfloat16
MODE_SLICES = 4
COLUMN_SLICES = 3
DENSE_SLICES = 5
CHUNK = 1024
PIECE = 512
INTERPRET = False


def iota(shape, axis):
    return lax.broadcasted_iota(jnp.int32, shape, axis)


def eye_mask(size):
    return iota((size, size), 0) == iota((size, size), 1)


def to_column(row):
    size = row.shape[1]
    return jnp.sum(jnp.where(eye_mask(size), row, 0.0), axis=1, keepdims=True)


def to_row(column):
    size = column.shape[0]
    return jnp.sum(jnp.where(eye_mask(size), column, 0.0), axis=0, keepdims=True)


def two_sum(a, b):
    total = a + b
    part = total - a
    return total, (a - (total - part)) + (b - part)


def split(a):
    scaled = a * 4097.0
    high = scaled - (scaled - a)
    return high, a - high


def two_product(a, b):
    product = a * b
    a_high, a_low = split(a)
    b_high, b_low = split(b)
    error = ((a_high * b_high - product) + a_high * b_low + a_low * b_high) + a_low * b_low
    return product, error


def power_of_two(bound):
    rest = bound
    scale = jnp.full_like(bound, 2.0)
    inverse = jnp.full_like(bound, 0.5)
    for step in (64, 32, 16, 8, 4, 2, 1):
        up, down = float(2.0**step), float(2.0**-step)
        large = rest >= up
        rest = jnp.where(large, rest * down, rest)
        scale = jnp.where(large, scale * up, scale)
        inverse = jnp.where(large, inverse * down, inverse)
    for step in (32, 16, 8, 4, 2, 1):
        up, down = float(2.0**step), float(2.0**-step)
        small = rest < 2.0 * down
        rest = jnp.where(small, rest * up, rest)
        scale = jnp.where(small, scale * down, scale)
        inverse = jnp.where(small, inverse * up, inverse)
    return scale, inverse


def slices_of(high, low, inverse, count):
    rest = high * (inverse * 128.0)
    out = []
    for index in range(count):
        if index == 2 and low is not None:
            rest = rest + low * (inverse * (128.0 * 65536.0))
        whole = jnp.round(rest)
        out.append(whole)
        if index + 1 < count:
            rest = (rest - whole) * 256.0
    return out


def dot_nt(a, b):
    return lax.dot_general(a, b, (((1,), (1,)), ((), ())), preferred_element_type=F32)


def levels_of(products, size, level_count):
    out = []
    for level in range(level_count):
        total = None
        for j, product in enumerate(products):
            i = level - j
            if 0 <= i and (i + 1) * size <= product.shape[0]:
                block = product[i * size : (i + 1) * size]
                total = block if total is None else total + block
        out.append(total)
    return out


def combine(leading, rest):
    high, low = leading[0], None
    for part in leading[1:]:
        high, error = two_sum(high, part)
        low = error if low is None else low + error
    tail = None
    for level in reversed(rest):
        tail = level if tail is None else level + tail * (1.0 / 256.0)
    tail = tail * (1.0 / 256.0)
    low = tail if low is None else low + tail
    return two_sum(high, low)


def long_gram(left_ref, left_size, right_ref, right_size, right_count, level_count):
    left_count = left_ref.shape[0] // left_size
    leading, rest = [], None
    for start in range(0, left_ref.shape[1], CHUNK):
        products = []
        for j in range(right_count):
            rows = min(left_count, level_count - j) * left_size
            products.append(
                dot_nt(
                    left_ref[0:rows, start : start + CHUNK],
                    right_ref[j * right_size : (j + 1) * right_size, start : start + CHUNK],
                )
            )
        levels = levels_of(products, left_size, level_count)
        leading.append(levels[0])
        rest = levels[1:] if rest is None else [a + b for a, b in zip(rest, levels[1:])]
    return combine(leading, rest)


def modes_kernel(basis_ref, parts_ref, scale_ref, pair_ref, gram_ref):
    size, lanes = basis_ref.shape
    bound = jnp.zeros((size, 1), F32)
    for start in range(0, lanes, CHUNK):
        bound = jnp.maximum(bound, jnp.max(jnp.abs(basis_ref[:, start : start + CHUNK]), axis=1, keepdims=True))
    scale, inverse = power_of_two(bound)
    scale_ref[...] = scale
    for start in range(0, lanes, PIECE):
        block = basis_ref[:, start : start + PIECE]
        for index, part in enumerate(slices_of(block, None, inverse, MODE_SLICES)):
            parts_ref[index * size : (index + 1) * size, start : start + PIECE] = part.astype(BF16)
        rounded = block.astype(BF16)
        pair_ref[0:size, start : start + PIECE] = rounded
        pair_ref[size : 2 * size, start : start + PIECE] = (block - rounded.astype(F32)).astype(BF16)
    high, low = long_gram(parts_ref, size, parts_ref, size, MODE_SLICES, MODE_SLICES)
    factor = scale * (1.0 / 16384.0)
    across = to_row(scale)
    gram_ref[0] = high * factor * across
    gram_ref[1] = low * factor * across


def columns_kernel(ids_ref, archive_ref, parts_ref, scale_ref, gram_ref, columns_ref, packed_ref, slices):
    count = ids_ref.shape[0]
    total, lanes = archive_ref.shape
    modes = scale_ref.shape[0]
    picker = jnp.where(ids_ref[...] == iota((count, total), 1), 1.0, 0.0).astype(BF16)
    bound = jnp.zeros((count, 1), F32)
    for start in range(0, lanes, PIECE):
        block = jnp.dot(picker, archive_ref[:, start : start + PIECE], preferred_element_type=F32)
        columns_ref[:, start : start + PIECE] = block.astype(BF16)
        bound = jnp.maximum(bound, jnp.max(jnp.abs(block), axis=1, keepdims=True))
    scale, inverse = power_of_two(bound)
    for start in range(0, lanes, PIECE):
        block = columns_ref[:, start : start + PIECE].astype(F32)
        for index, part in enumerate(slices_of(block, None, inverse, COLUMN_SLICES)):
            slices[index * count : (index + 1) * count, start : start + PIECE] = part.astype(BF16)
    across = to_row(scale)
    p_high, p_low = long_gram(parts_ref, modes, slices, count, COLUMN_SLICES, 4)
    factor = scale_ref[...] * (1.0 / 16384.0)
    p_high, p_low = p_high * factor * across, p_low * factor * across
    c_high, c_low = long_gram(slices, count, slices, count, COLUMN_SLICES, 4)
    factor = scale * (1.0 / 16384.0)
    c_high, c_low = c_high * factor * across, c_low * factor * across
    g_high, g_low = gram_ref[0], gram_ref[1]
    n = count
    packed_ref[0:n, :] = jnp.concatenate([p_high[0:n], p_low[0:n], p_high[n:], p_low[n:]], axis=1)
    packed_ref[n : 2 * n, :] = jnp.concatenate([c_high, c_low, g_high[0:n, 0:n], g_low[0:n, 0:n]], axis=1)
    packed_ref[2 * n :, :] = jnp.concatenate(
        [g_high[n:, 0:n], g_low[n:, 0:n], g_high[n:, n:], g_low[n:, n:]], axis=1
    )


def sum_pairs(load, count):
    high = load(0)
    error = jnp.zeros_like(high)
    for index in range(1, count):
        high, part = two_sum(high, load(index))
        error = error + part
    odd = (iota(high.shape, 1) // 32) % 2 == 1
    return jnp.where(odd, high + pltpu.roll(error, 32, 1), high)


def half_kernel(place_ref, both_ref, out_ref):
    copies, rows, _ = out_ref.shape
    start = pl.multiple_of(place_ref[0] * rows, 8)
    total = sum_pairs(lambda index: both_ref[index, pl.ds(start, rows), :], both_ref.shape[0])
    for index in range(copies):
        out_ref[index] = total


def sum_kernel(parts_ref, out_ref):
    total = sum_pairs(lambda index: parts_ref[index], parts_ref.shape[0])
    if len(out_ref.shape) == 2:
        out_ref[...] = total
    else:
        for index in range(out_ref.shape[0]):
            out_ref[index] = total


def high_dot(a, b):
    return jnp.dot(a, b, precision=HIGH, preferred_element_type=F32)


def slice_product(left, right, level_count):
    size = left[0].shape[0]
    stacked = jnp.concatenate(left, axis=0).astype(BF16)
    products = []
    for j, part in enumerate(right):
        rows = (level_count - j) * size
        products.append(jnp.dot(stacked[0:rows], part.astype(BF16), preferred_element_type=F32))
    levels = levels_of(products, size, level_count)
    return combine(levels[0:1], levels[1:])


def triangle(high, low):
    size = high.shape[0]
    rows = iota((size, size), 0)
    for j in range(size - 1):
        row_high, row_low = high[j : j + 1, :], low[j : j + 1, :]
        below = iota((size, 1), 0) > j
        col_high = jnp.where(below, high[:, j : j + 1], 0.0)
        col_low = jnp.where(below, low[:, j : j + 1], 0.0)
        d_high, d_low = row_high[:, j : j + 1], row_low[:, j : j + 1]
        q_high = 1.0 / d_high
        p_high, p_low = two_product(d_high, q_high)
        q_low = q_high * (((1.0 - p_high) - p_low) - d_low * q_high)
        w_high, w_error = two_product(col_high, q_high)
        w_low = w_error + (col_high * q_low + col_low * q_high)
        u_high, u_error = two_product(w_high, row_high)
        u_low = u_error + (w_high * row_low + w_low * row_high)
        s_high, s_error = two_sum(high, -u_high)
        s_low = s_error + (low - u_low)
        high = s_high + s_low
        low = s_low - (high - s_high)
    pivots = jnp.sum(jnp.where(eye_mask(size), high, 0.0), axis=1, keepdims=True)
    return jnp.where(iota((size, size), 1) >= rows, high * lax.rsqrt(pivots), 0.0)


def dense(packed, values, total_rows):
    n = packed.shape[0] // 3
    m = 2 * n
    width = m + n
    square_scale = 1.0 / total_rows
    scale = math.sqrt(square_scale)

    def block(row, lane):
        return packed[row * n : (row + 1) * n, lane * n : (lane + 1) * n]

    p_high = jnp.concatenate([block(0, 0), block(0, 2)], axis=0)
    p_low = jnp.concatenate([block(0, 1), block(0, 3)], axis=0)
    p_high, p_low = two_sum(p_high, p_low)
    c_high, c_low = two_sum(block(1, 0), block(1, 1))
    g_high = jnp.concatenate(
        [
            jnp.concatenate([block(1, 2), block(2, 0).T], axis=1),
            jnp.concatenate([block(2, 0), block(2, 2)], axis=1),
        ],
        axis=0,
    )
    g_low = jnp.concatenate(
        [
            jnp.concatenate([block(1, 3), block(2, 1).T], axis=1),
            jnp.concatenate([block(2, 1), block(2, 3)], axis=1),
        ],
        axis=0,
    )
    eye_m = jnp.where(eye_mask(m), 1.0, 0.0)
    t_high, t_error = two_sum(2.0 * eye_m, -g_high)
    t_high, t_low = two_sum(t_high, t_error - g_low)

    t_scale, t_inverse = power_of_two(jnp.max(jnp.max(jnp.abs(t_high), axis=1, keepdims=True), axis=0, keepdims=True))
    p_scale, p_inverse = power_of_two(jnp.max(jnp.abs(p_high), axis=0, keepdims=True))
    p_slices = slices_of(p_high, p_low, p_inverse, DENSE_SLICES)
    h_high, h_low = slice_product(slices_of(t_high, t_low, t_inverse, DENSE_SLICES), p_slices, DENSE_SLICES)
    h_scale, h_inverse = power_of_two(jnp.max(jnp.abs(h_high), axis=0, keepdims=True))
    pt_slices = [part.T for part in p_slices]
    q_high, q_low = slice_product(pt_slices, slices_of(h_high, h_low, h_inverse, DENSE_SLICES), DENSE_SLICES)
    factor = to_column(p_scale) * (1.0 / 16384.0)
    across = h_scale * (p_scale * (t_scale * (1.0 / 16384.0)))
    q_high, q_low = q_high * factor * across, q_low * factor * across
    r_high, r_error = two_sum(c_high, -q_high)
    one_high, one_low = two_sum(r_high, r_error + (c_low - q_low))

    eye_n = eye_mask(n)
    own = jnp.sum(jnp.where(eye_n, one_high, 0.0), axis=0, keepdims=True)
    energy = jnp.sum(jnp.where(eye_n, c_high, 0.0), axis=0, keepdims=True)
    novelty = own / energy

    values_column = to_column(values)
    projection = p_high * scale
    gram = one_high * square_scale
    turned = projection.T
    mixed = projection * values_column
    kernel_top = jnp.concatenate([eye_m * (values_column * values_column), mixed], axis=1)
    kernel_low = jnp.concatenate([mixed.T, high_dot(turned, projection) + gram], axis=1)
    inner = jnp.concatenate([kernel_top, kernel_low], axis=0)
    eye_w = jnp.where(eye_mask(width), 1.0, 0.0)
    total = jnp.sum(jnp.sum(inner * eye_w, axis=1, keepdims=True), axis=0, keepdims=True)
    shifted = (inner - (total / width) * eye_w) / total
    slope = eye_w
    origin = -1.0 / width
    for _ in range(NEWTON):
        squared = high_dot(shifted, shifted)
        divided = (origin * origin) * eye_w + origin * shifted + squared
        slope = 1.5 * slope - 0.5 * high_dot(slope, divided)
        shifted = 1.5 * shifted - 0.5 * high_dot(shifted, squared)
        origin = 1.5 * origin - 0.5 * origin * origin * origin
    blend = 0.5 * (eye_w + shifted)
    slope = slope * (0.5 / total)

    upper = triangle(one_high, one_low) * scale
    core = jnp.concatenate(
        [
            jnp.concatenate([eye_m * values_column, projection], axis=1),
            jnp.concatenate([jnp.zeros((n, m), F32), upper], axis=1),
        ],
        axis=0,
    )
    half = high_dot(core, slope)
    projector = (0.5 * (1.0 + origin)) * eye_w + lax.dot_general(
        half, core, (((1,), (1,)), ((), ())), precision=HIGH, preferred_element_type=F32
    )
    weights = jnp.concatenate([blend[:, 0:m] * (values * math.sqrt(total_rows)), blend[:, m:]], axis=1)
    return weights, projector, novelty


def finish_kernel(total_rows, packed_ref, values_ref, pair_ref, columns_ref, filtered_ref, projector_ref, novelty_ref, left):
    modes = values_ref.shape[1]

    @pl.when(pl.program_id(0) == 0)
    def _():
        weights, projector, novelty = dense(packed_ref[...], values_ref[...], total_rows)
        projector_ref[...] = projector
        novelty_ref[...] = novelty
        rounded = weights.astype(BF16)
        rest = (weights - rounded.astype(F32)).astype(BF16)
        left[...] = jnp.concatenate(
            [rounded[:, 0:modes], rounded[:, 0:modes], rest[:, 0:modes], rounded[:, modes:], rest[:, modes:]], axis=1
        )

    lanes = filtered_ref.shape[1]
    for start in range(0, lanes, 256):
        where = slice(start, start + 256)
        first, second, third = pair_ref[0:modes, where], pair_ref[modes:, where], columns_ref[:, where]
        right = jnp.concatenate([first, second, first, third, third], axis=0)
        filtered_ref[:, where] = jnp.dot(left[...], right, preferred_element_type=F32)


def vmem(count):
    return [pl.BlockSpec(memory_space=pltpu.VMEM)] * count


def shape(dims, dtype=F32):
    return jax.ShapeDtypeStruct(dims, dtype)


def prepare(basis):
    modes, lanes = basis.shape
    return pl.pallas_call(
        modes_kernel,
        out_shape=(
            shape((MODE_SLICES * modes, lanes), BF16),
            shape((modes, 1)),
            shape((2 * modes, lanes), BF16),
            shape((2, modes, modes)),
        ),
        in_specs=vmem(1),
        out_specs=tuple(vmem(4)),
        interpret=INTERPRET,
        name="modes",
    )(basis)


def gather(ids, everything, parts, scale, gram):
    count, lanes = ids.shape[0], everything.shape[1]
    return pl.pallas_call(
        columns_kernel,
        out_shape=(shape((count, lanes), BF16), shape((3 * count, 128))),
        in_specs=vmem(5),
        out_specs=tuple(vmem(2)),
        scratch_shapes=[pltpu.VMEM((COLUMN_SLICES * count, lanes), BF16)],
        interpret=INTERPRET,
        name="columns",
    )(ids, everything, parts, scale, gram)


def take_half(place, both, copies):
    rows = both.shape[1] // 2
    return pl.pallas_call(
        half_kernel,
        out_shape=shape((copies, rows, 128)),
        in_specs=[pl.BlockSpec(memory_space=pltpu.SMEM)] + vmem(1),
        out_specs=vmem(1)[0],
        interpret=INTERPRET,
        name="half",
    )(place, both)


def add_up(parts, copies):
    rows = parts.shape[1]
    return pl.pallas_call(
        sum_kernel,
        out_shape=shape((rows, 128) if copies is None else (copies, rows, 128)),
        in_specs=vmem(1),
        out_specs=vmem(1)[0],
        interpret=INTERPRET,
        name="add",
    )(parts)


def finish(total_rows, packed, values, pair, columns):
    import functools

    modes, count, lanes = values.shape[1], columns.shape[0], columns.shape[1]
    width = modes + count
    steps = 4
    return pl.pallas_call(
        functools.partial(finish_kernel, total_rows),
        grid=(steps,),
        out_shape=(shape((width, lanes)), shape((width, width)), shape((1, count))),
        in_specs=[
            pl.BlockSpec((3 * count, 128), lambda i: (0, 0)),
            pl.BlockSpec((1, modes), lambda i: (0, 0)),
            pl.BlockSpec((2 * modes, lanes // steps), lambda i: (0, i)),
            pl.BlockSpec((count, lanes // steps), lambda i: (0, i)),
        ],
        out_specs=(
            pl.BlockSpec((width, lanes // steps), lambda i: (0, i)),
            pl.BlockSpec((width, width), lambda i: (0, 0)),
            pl.BlockSpec((1, count), lambda i: (0, 0)),
        ),
        scratch_shapes=[pltpu.VMEM((width, 256), BF16)],
        interpret=INTERPRET,
        name="finish",
    )(packed, values, pair, columns)


def exchange(copies, axes):
    return lax.all_to_all(copies, axes, 0, 0, tiled=True)


def per_device(basis, values, archive, window_ids):
    total_rows = basis.shape[1]
    for name in ALL:
        total_rows *= lax.axis_size(name)
    everything = lax.all_to_all(archive, ("x", "c"), split_axis=1, concat_axis=0, tiled=True)
    parts, scale, pair, gram = prepare(basis)
    columns, packed = gather(window_ids[:, None], everything, parts, scale, gram)
    both = lax.all_gather(packed, "c")
    plane = lax.axis_size("y") * lax.axis_size("x")
    place = lax.axis_index("c").astype(jnp.int32)[None]
    first = exchange(take_half(place, both, plane), ("y", "x"))
    second = exchange(add_up(first, lax.axis_size("z")), ("z",))
    packed = lax.all_gather(add_up(second, None), "c", tiled=True)
    filtered, projector, novelty = finish(total_rows, packed, values[None, :], pair, columns)
    return (filtered, projector, novelty.reshape(-1))


def solution(mesh):
    fine = Mesh(mesh.devices.reshape(8, 8, 4, 2), ALL)
    placed = (P(None, ALL), P(), P(("x", "c"), ("y", "z")), P())
    return jax.shard_map(
        per_device,
        mesh=fine,
        in_specs=placed,
        out_specs=(P(None, ALL), P(), P()),
        check_vma=False,
    )
```

```python
import functools
import math

import jax
import jax.numpy as jnp
from jax import lax
from jax.experimental import pallas as pl
from jax.experimental.pallas import tpu as pltpu
from jax.sharding import Mesh, PartitionSpec as P

NEWTON = 10
HIGH = lax.Precision.HIGHEST
ALL = ("y", "z", "x", "c")
F32 = jnp.float32
BF16 = jnp.bfloat16
MODE_SLICES = 4
COLUMN_SLICES = 3
DENSE_SLICES = 5
CHUNK = 1024
PIECE = 512
INTERPRET = False


def iota(shape, axis):
    return lax.broadcasted_iota(jnp.int32, shape, axis)


def eye_mask(size):
    return iota((size, size), 0) == iota((size, size), 1)


def to_column(row):
    size = row.shape[1]
    return jnp.sum(jnp.where(eye_mask(size), row, 0.0), axis=1, keepdims=True)


def to_row(column):
    size = column.shape[0]
    return jnp.sum(jnp.where(eye_mask(size), column, 0.0), axis=0, keepdims=True)


def two_sum(a, b):
    total = a + b
    part = total - a
    return total, (a - (total - part)) + (b - part)


def split(a):
    scaled = a * 4097.0
    high = scaled - (scaled - a)
    return high, a - high


def two_product(a, b):
    product = a * b
    a_high, a_low = split(a)
    b_high, b_low = split(b)
    error = ((a_high * b_high - product) + a_high * b_low + a_low * b_high) + a_low * b_low
    return product, error


def power_of_two(bound):
    rest = bound
    scale = jnp.full_like(bound, 2.0)
    inverse = jnp.full_like(bound, 0.5)
    for step in (64, 32, 16, 8, 4, 2, 1):
        up, down = float(2.0**step), float(2.0**-step)
        large = rest >= up
        rest = jnp.where(large, rest * down, rest)
        scale = jnp.where(large, scale * up, scale)
        inverse = jnp.where(large, inverse * down, inverse)
    for step in (32, 16, 8, 4, 2, 1):
        up, down = float(2.0**step), float(2.0**-step)
        small = rest < 2.0 * down
        rest = jnp.where(small, rest * up, rest)
        scale = jnp.where(small, scale * down, scale)
        inverse = jnp.where(small, inverse * up, inverse)
    return scale, inverse


def slices_of(high, low, inverse, count):
    rest = high * (inverse * 128.0)
    out = []
    for index in range(count):
        if index == 2 and low is not None:
            rest = rest + low * (inverse * (128.0 * 65536.0))
        whole = jnp.round(rest)
        out.append(whole)
        if index + 1 < count:
            rest = (rest - whole) * 256.0
    return out


def dot_nt(a, b):
    return lax.dot_general(a, b, (((1,), (1,)), ((), ())), preferred_element_type=F32)


def levels_of(products, size, level_count):
    out = []
    for level in range(level_count):
        total = None
        for j, product in enumerate(products):
            i = level - j
            if 0 <= i and (i + 1) * size <= product.shape[0]:
                block = product[i * size : (i + 1) * size]
                total = block if total is None else total + block
        out.append(total)
    return out


def combine(leading, rest):
    high, low = leading[0], None
    for part in leading[1:]:
        high, error = two_sum(high, part)
        low = error if low is None else low + error
    tail = None
    for level in reversed(rest):
        tail = level if tail is None else level + tail * (1.0 / 256.0)
    tail = tail * (1.0 / 256.0)
    low = tail if low is None else low + tail
    return two_sum(high, low)


def long_gram(left_ref, left_size, right_ref, right_size, right_count, level_count):
    left_count = left_ref.shape[0] // left_size
    leading, rest = [], None
    for start in range(0, left_ref.shape[1], CHUNK):
        products = []
        for j in range(right_count):
            rows = min(left_count, level_count - j) * left_size
            products.append(
                dot_nt(
                    left_ref[0:rows, start : start + CHUNK],
                    right_ref[j * right_size : (j + 1) * right_size, start : start + CHUNK],
                )
            )
        levels = levels_of(products, left_size, level_count)
        leading.append(levels[0])
        rest = levels[1:] if rest is None else [a + b for a, b in zip(rest, levels[1:])]
    return combine(leading, rest)


def modes_kernel(share, basis_ref, parts_ref, scale_ref, pair_ref, gram_ref):
    size, lanes = basis_ref.shape
    bound = jnp.zeros((size, 1), F32)
    for start in range(0, lanes, CHUNK):
        bound = jnp.maximum(bound, jnp.max(jnp.abs(basis_ref[:, start : start + CHUNK]), axis=1, keepdims=True))
    scale, inverse = power_of_two(bound)
    scale_ref[...] = scale
    for start in range(0, lanes, PIECE):
        block = basis_ref[:, start : start + PIECE]
        for index, part in enumerate(slices_of(block, None, inverse, MODE_SLICES)):
            parts_ref[index * size : (index + 1) * size, start : start + PIECE] = part.astype(BF16)
        rounded = block.astype(BF16)
        pair_ref[0:size, start : start + PIECE] = rounded
        pair_ref[size : 2 * size, start : start + PIECE] = (block - rounded.astype(F32)).astype(BF16)
    high, low = long_gram(parts_ref, size, parts_ref, size, MODE_SLICES, MODE_SLICES)
    factor = scale * (1.0 / 16384.0)
    across = to_row(scale)
    gram_ref[...] = (high * factor * across - jnp.where(eye_mask(size), share, 0.0)) + low * factor * across


def cyclic(size):
    rows, lanes = iota((size, size), 0), iota((size, size), 1)
    return (lanes == rows + 1) | ((rows == size - 1) & (lanes == 0))


def columns_kernel(
    ids_ref, archive_ref, parts_hbm, scale_ref, gram_ref, columns_ref, packed_ref, slices, parts, arrived
):
    count = ids_ref.shape[0]
    total, lanes = archive_ref.shape
    modes = scale_ref.shape[0]
    starts = range(0, lanes, CHUNK)
    copies = [
        pltpu.make_async_copy(
            parts_hbm.at[:, pl.ds(start, CHUNK)], parts.at[:, pl.ds(start, CHUNK)], arrived.at[index]
        )
        for index, start in enumerate(starts)
    ]
    for copy in copies:
        copy.start()
    picker = jnp.where(ids_ref[...] == iota((count, total), 1), 1.0, 0.0).astype(BF16)
    bound = jnp.zeros((count, 1), F32)
    for start in range(0, lanes, PIECE):
        block = jnp.dot(picker, archive_ref[:, start : start + PIECE], preferred_element_type=F32)
        columns_ref[:, start : start + PIECE] = block.astype(BF16)
        bound = jnp.maximum(bound, jnp.max(jnp.abs(block), axis=1, keepdims=True))
    scale, inverse = power_of_two(bound)
    for start in range(0, lanes, PIECE):
        block = columns_ref[:, start : start + PIECE].astype(F32)
        for index, part in enumerate(slices_of(block, None, inverse, COLUMN_SLICES)):
            slices[index * count : (index + 1) * count, start : start + PIECE] = part.astype(BF16)

    whole, lead_p, lead_c = None, [], []
    height = MODE_SLICES * modes
    for start, copy in zip(starts, copies):
        copy.wait()
        right = slices[:, start : start + CHUNK]
        product = dot_nt(jnp.concatenate([parts[:, start : start + CHUNK], right], axis=0), right)
        lead_p.append(product[0:modes, 0:count])
        lead_c.append(product[height : height + count, 0:count])
        whole = product if whole is None else whole + product
    by_slice = [whole[:, j * count : (j + 1) * count] for j in range(COLUMN_SLICES)]
    last = MODE_SLICES + COLUMN_SLICES - 2
    p_high, p_low = combine(lead_p, levels_of([part[0:height] for part in by_slice], modes, last)[1:])
    last = 2 * COLUMN_SLICES - 1
    c_high, c_low = combine(lead_c, levels_of([part[height:] for part in by_slice], count, last)[1:])
    across = to_row(scale)
    factor = scale_ref[...] * (1.0 / 16384.0)
    p_high, p_low = p_high * factor * across, p_low * factor * across
    factor = scale * (1.0 / 16384.0)
    c_high, c_low = c_high * factor * across, c_low * factor * across
    n = count
    gram = gram_ref[...]
    last_block = gram[n:, n:]
    last_diagonal = jnp.sum(jnp.where(eye_mask(n), last_block, 0.0), axis=1, keepdims=True)
    c_low = jnp.where(cyclic(n), last_diagonal, c_low)
    corner = jnp.where(iota((n, n), 0) >= iota((n, n), 1), gram[0:n, 0:n], last_block)
    top = jnp.concatenate([p_high[0:n], p_low[0:n], p_high[n:], p_low[n:]], axis=1)
    low = jnp.concatenate([c_high, c_low, gram[n:, 0:n], corner], axis=1)
    for index in range(packed_ref.shape[0]):
        packed_ref[index, 0:n, :] = top
        packed_ref[index, n:, :] = low


def sum_pairs(parts_ref):
    high = parts_ref[0]
    error = jnp.zeros_like(high)
    for index in range(1, parts_ref.shape[0]):
        high, part = two_sum(high, parts_ref[index])
        error = error + part
    n = high.shape[0] // 2
    rows, lanes = iota(high.shape, 0), iota(high.shape, 1)
    top_takes = (rows < n) & ((lanes // n) % 2 == 1)
    row, lane = rows - n, lanes - n
    special = (lane == row + 1) | ((row == n - 1) & (lane == 0))
    takes = top_takes | ((row >= 0) & (lane >= 0) & (lane < n) & jnp.logical_not(special))
    return jnp.where(takes, high + pltpu.roll(error, n, 1), high)


def sum_kernel(parts_ref, out_ref):
    total = sum_pairs(parts_ref)
    for index in range(out_ref.shape[0]):
        out_ref[index] = total


def high_dot(a, b):
    return jnp.dot(a, b, precision=HIGH, preferred_element_type=F32)


def slice_product(left, right, level_count):
    size = left[0].shape[0]
    stacked = jnp.concatenate(left, axis=0).astype(BF16)
    products = []
    for j, part in enumerate(right):
        rows = (level_count - j) * size
        products.append(jnp.dot(stacked[0:rows], part.astype(BF16), preferred_element_type=F32))
    levels = levels_of(products, size, level_count)
    return combine(levels[0:1], levels[1:])


def triangle(high, low):
    size = high.shape[0]
    rows = iota((size, size), 0)
    for j in range(size - 1):
        row_high, row_low = high[j : j + 1, :], low[j : j + 1, :]
        below = iota((size, 1), 0) > j
        col_high = jnp.where(below, high[:, j : j + 1], 0.0)
        col_low = jnp.where(below, low[:, j : j + 1], 0.0)
        d_high, d_low = row_high[:, j : j + 1], row_low[:, j : j + 1]
        q_high = 1.0 / d_high
        p_high, p_low = two_product(d_high, q_high)
        q_low = q_high * (((1.0 - p_high) - p_low) - d_low * q_high)
        w_high, w_error = two_product(col_high, q_high)
        w_low = w_error + (col_high * q_low + col_low * q_high)
        u_high, u_error = two_product(w_high, row_high)
        u_low = u_error + (w_high * row_low + w_low * row_high)
        s_high, s_error = two_sum(high, -u_high)
        s_low = s_error + (low - u_low)
        high = s_high + s_low
        low = s_low - (high - s_high)
    pivots = jnp.sum(jnp.where(eye_mask(size), high, 0.0), axis=1, keepdims=True)
    return jnp.where(iota((size, size), 1) >= rows, high * lax.rsqrt(pivots), 0.0)


def dense(packed, values, total_rows):
    n = packed.shape[0] // 2
    m = 2 * n
    width = m + n
    square_scale = 1.0 / total_rows
    scale = math.sqrt(square_scale)

    def block(row, lane):
        return packed[row * n : (row + 1) * n, lane * n : (lane + 1) * n]

    p_high = jnp.concatenate([block(0, 0), block(0, 2)], axis=0)
    p_low = jnp.concatenate([block(0, 1), block(0, 3)], axis=0)
    p_high, p_low = two_sum(p_high, p_low)
    stored, corner, side = block(1, 1), block(1, 3), block(1, 2)
    special = cyclic(n)
    last_diagonal = jnp.sum(jnp.where(special, stored, 0.0), axis=1, keepdims=True)
    c_high, c_low = two_sum(block(1, 0), jnp.where(special, stored.T, stored))
    rows, lanes = iota((n, n), 0), iota((n, n), 1)
    turned_corner = corner.T
    first_block = jnp.where(rows >= lanes, corner, turned_corner)
    last_block = jnp.where(rows > lanes, turned_corner, jnp.where(rows < lanes, corner, last_diagonal))
    excess = jnp.concatenate(
        [jnp.concatenate([first_block, side.T], axis=1), jnp.concatenate([side, last_block], axis=1)], axis=0
    )
    eye_m = jnp.where(eye_mask(m), 1.0, 0.0)
    t_high, t_low = two_sum(eye_m, -excess)

    t_scale, t_inverse = power_of_two(jnp.max(jnp.max(jnp.abs(t_high), axis=1, keepdims=True), axis=0, keepdims=True))
    p_scale, p_inverse = power_of_two(jnp.max(jnp.abs(p_high), axis=0, keepdims=True))
    p_slices = slices_of(p_high, p_low, p_inverse, DENSE_SLICES)
    h_high, h_low = slice_product(slices_of(t_high, t_low, t_inverse, DENSE_SLICES), p_slices, DENSE_SLICES)
    h_scale, h_inverse = power_of_two(jnp.max(jnp.abs(h_high), axis=0, keepdims=True))
    pt_slices = [part.T for part in p_slices]
    q_high, q_low = slice_product(pt_slices, slices_of(h_high, h_low, h_inverse, DENSE_SLICES), DENSE_SLICES)
    factor = to_column(p_scale) * (1.0 / 16384.0)
    across = h_scale * (p_scale * (t_scale * (1.0 / 16384.0)))
    q_high, q_low = q_high * factor * across, q_low * factor * across
    r_high, r_error = two_sum(c_high, -q_high)
    one_high, one_low = two_sum(r_high, r_error + (c_low - q_low))

    eye_n = eye_mask(n)
    own = jnp.sum(jnp.where(eye_n, one_high, 0.0), axis=0, keepdims=True)
    energy = jnp.sum(jnp.where(eye_n, c_high, 0.0), axis=0, keepdims=True)
    novelty = own / energy

    values_column = to_column(values)
    projection = p_high * scale
    gram = one_high * square_scale
    turned = projection.T
    mixed = projection * values_column
    kernel_top = jnp.concatenate([eye_m * (values_column * values_column), mixed], axis=1)
    kernel_low = jnp.concatenate([mixed.T, high_dot(turned, projection) + gram], axis=1)
    inner = jnp.concatenate([kernel_top, kernel_low], axis=0)
    eye_w = jnp.where(eye_mask(width), 1.0, 0.0)
    total = jnp.sum(jnp.sum(inner * eye_w, axis=1, keepdims=True), axis=0, keepdims=True)
    shifted = (inner - (total / width) * eye_w) / total
    slope = eye_w
    origin = -1.0 / width
    for _ in range(NEWTON):
        squared = high_dot(shifted, shifted)
        divided = (origin * origin) * eye_w + origin * shifted + squared
        slope = 1.5 * slope - 0.5 * high_dot(slope, divided)
        shifted = 1.5 * shifted - 0.5 * high_dot(shifted, squared)
        origin = 1.5 * origin - 0.5 * origin * origin * origin
    blend = 0.5 * (eye_w + shifted)
    slope = slope * (0.5 / total)

    upper = triangle(one_high, one_low) * scale
    core = jnp.concatenate(
        [
            jnp.concatenate([eye_m * values_column, projection], axis=1),
            jnp.concatenate([jnp.zeros((n, m), F32), upper], axis=1),
        ],
        axis=0,
    )
    half = high_dot(core, slope)
    projector = (0.5 * (1.0 + origin)) * eye_w + lax.dot_general(
        half, core, (((1,), (1,)), ((), ())), precision=HIGH, preferred_element_type=F32
    )
    weights = jnp.concatenate([blend[:, 0:m] * (values * math.sqrt(total_rows)), blend[:, m:]], axis=1)
    return weights, projector, novelty


def finish_kernel(
    total_rows,
    packed_ref,
    values_ref,
    pair_hbm,
    columns_hbm,
    filtered_hbm,
    projector_ref,
    novelty_ref,
    pair,
    columns,
    filtered,
    arrived,
    left_sem,
):
    modes = values_ref.shape[1]
    lanes = pair.shape[1]
    loads = [
        pltpu.make_async_copy(pair_hbm, pair, arrived.at[0]),
        pltpu.make_async_copy(columns_hbm, columns, arrived.at[1]),
    ]
    for load in loads:
        load.start()
    weights, projector, novelty = dense(sum_pairs(packed_ref), values_ref[...], total_rows)
    rounded = weights.astype(BF16)
    rest = (weights - rounded.astype(F32)).astype(BF16)
    left = jnp.concatenate(
        [rounded[:, 0:modes], rounded[:, 0:modes], rest[:, 0:modes], rounded[:, modes:], rest[:, modes:]], axis=1
    )
    for load in loads:
        load.wait()
    stores = []
    for start in range(0, lanes, PIECE):
        where = slice(start, start + PIECE)
        first, second, third = pair[0:modes, where], pair[modes:, where], columns[:, where]
        right = jnp.concatenate([first, second, first, third, third], axis=0)
        filtered[:, where] = jnp.dot(left, right, preferred_element_type=F32)
        store = pltpu.make_async_copy(
            filtered.at[:, pl.ds(start, PIECE)], filtered_hbm.at[:, pl.ds(start, PIECE)], left_sem.at[len(stores)]
        )
        store.start()
        stores.append(store)
    projector_ref[...] = projector
    novelty_ref[...] = novelty
    for store in stores:
        store.wait()


def vmem(count):
    return [pl.BlockSpec(memory_space=pltpu.VMEM)] * count


def shape(dims, dtype=F32):
    return jax.ShapeDtypeStruct(dims, dtype)


def prepare(basis, share):
    modes, lanes = basis.shape
    return pl.pallas_call(
        functools.partial(modes_kernel, share),
        out_shape=(
            shape((MODE_SLICES * modes, lanes), BF16),
            shape((modes, 1)),
            shape((2 * modes, lanes), BF16),
            shape((modes, modes)),
        ),
        in_specs=vmem(1),
        out_specs=tuple(vmem(4)),
        interpret=INTERPRET,
        name="modes",
    )(basis)


def gather(ids, everything, parts, scale, gram, copies):
    count, lanes = ids.shape[0], everything.shape[1]
    return pl.pallas_call(
        columns_kernel,
        out_shape=(shape((count, lanes), BF16), shape((copies, 2 * count, 128))),
        in_specs=vmem(2) + [pl.BlockSpec(memory_space=pl.ANY)] + vmem(2),
        out_specs=tuple(vmem(2)),
        scratch_shapes=[
            pltpu.VMEM((COLUMN_SLICES * count, lanes), BF16),
            pltpu.VMEM(parts.shape, BF16),
            pltpu.SemaphoreType.DMA((lanes // CHUNK,)),
        ],
        interpret=INTERPRET,
        name="columns",
    )(ids, everything, parts, scale, gram)


def add_up(parts, copies):
    return pl.pallas_call(
        sum_kernel,
        out_shape=shape((copies,) + parts.shape[1:]),
        in_specs=vmem(1),
        out_specs=vmem(1)[0],
        interpret=INTERPRET,
        name="add",
    )(parts)


def finish(total_rows, packed, values, pair, columns):
    modes, count, lanes = values.shape[1], columns.shape[0], columns.shape[1]
    width = modes + count
    anywhere = pl.BlockSpec(memory_space=pl.ANY)
    return pl.pallas_call(
        functools.partial(finish_kernel, total_rows),
        out_shape=(shape((width, lanes)), shape((width, width)), shape((1, count))),
        in_specs=vmem(2) + [anywhere, anywhere],
        out_specs=(anywhere,) + tuple(vmem(2)),
        scratch_shapes=[
            pltpu.VMEM(pair.shape, BF16),
            pltpu.VMEM(columns.shape, BF16),
            pltpu.VMEM((width, lanes), F32),
            pltpu.SemaphoreType.DMA((2,)),
            pltpu.SemaphoreType.DMA((lanes // PIECE,)),
        ],
        interpret=INTERPRET,
        name="finish",
    )(packed, values, pair, columns)


def exchange(copies, axes):
    return near(lax.all_to_all(copies, axes, 0, 0, tiled=True))


def near(array):
    return pltpu.with_memory_space_constraint(array, pltpu.VMEM)


def per_device(basis, values, archive, window_ids):
    devices = 1
    for name in ALL:
        devices *= lax.axis_size(name)
    total_rows = basis.shape[1] * devices
    everything = near(lax.all_to_all(archive, ("x", "c"), split_axis=1, concat_axis=0, tiled=True))
    parts, scale, pair, gram = prepare(basis, 1.0 / devices)
    columns, packed = gather(window_ids[:, None], everything, parts, scale, gram, lax.axis_size("y"))
    packed = add_up(exchange(packed, ("y",)), lax.axis_size("z"))
    packed = add_up(exchange(packed, ("z",)), lax.axis_size("x") * lax.axis_size("c"))
    packed = exchange(packed, ("x", "c"))
    filtered, projector, novelty = finish(total_rows, packed, values[None, :], pair, columns)
    return (filtered, projector, novelty.reshape(-1))


def solution(mesh):
    fine = Mesh(mesh.devices.reshape(8, 8, 4, 2), ALL)
    placed = (P(None, ALL), P(), P(("x", "c"), ("y", "z")), P())
    return jax.shard_map(
        per_device,
        mesh=fine,
        in_specs=placed,
        out_specs=(P(None, ALL), P(), P()),
        check_vma=False,
    )
```

```python
import functools
import math

import jax
import jax.numpy as jnp
from jax import lax
from jax.experimental import pallas as pl
from jax.experimental.pallas import tpu as pltpu
from jax.sharding import Mesh, PartitionSpec as P

NEWTON = 10
HIGH = lax.Precision.HIGHEST
ALL = ("y", "z", "x", "c")
F32 = jnp.float32
BF16 = jnp.bfloat16
MODE_SLICES = 4
COLUMN_SLICES = 3
DENSE_SLICES = 5
CHUNK = 1024
PIECE = 512
INTERPRET = False


def iota(shape, axis):
    return lax.broadcasted_iota(jnp.int32, shape, axis)


def eye_mask(size):
    return iota((size, size), 0) == iota((size, size), 1)


def to_column(row):
    size = row.shape[1]
    return jnp.sum(jnp.where(eye_mask(size), row, 0.0), axis=1, keepdims=True)


def to_row(column):
    size = column.shape[0]
    return jnp.sum(jnp.where(eye_mask(size), column, 0.0), axis=0, keepdims=True)


def two_sum(a, b):
    total = a + b
    part = total - a
    return total, (a - (total - part)) + (b - part)


def split(a):
    scaled = a * 4097.0
    high = scaled - (scaled - a)
    return high, a - high


def two_product(a, b):
    product = a * b
    a_high, a_low = split(a)
    b_high, b_low = split(b)
    error = ((a_high * b_high - product) + a_high * b_low + a_low * b_high) + a_low * b_low
    return product, error


def power_of_two(bound):
    rest = bound
    scale = jnp.full_like(bound, 2.0)
    inverse = jnp.full_like(bound, 0.5)
    for step in (64, 32, 16, 8, 4, 2, 1):
        up, down = float(2.0**step), float(2.0**-step)
        large = rest >= up
        rest = jnp.where(large, rest * down, rest)
        scale = jnp.where(large, scale * up, scale)
        inverse = jnp.where(large, inverse * down, inverse)
    for step in (32, 16, 8, 4, 2, 1):
        up, down = float(2.0**step), float(2.0**-step)
        small = rest < 2.0 * down
        rest = jnp.where(small, rest * up, rest)
        scale = jnp.where(small, scale * down, scale)
        inverse = jnp.where(small, inverse * up, inverse)
    return scale, inverse


def slices_of(high, low, inverse, count):
    rest = high * (inverse * 128.0)
    out = []
    for index in range(count):
        if index == 2 and low is not None:
            rest = rest + low * (inverse * (128.0 * 65536.0))
        whole = jnp.round(rest)
        out.append(whole)
        if index + 1 < count:
            rest = (rest - whole) * 256.0
    return out


def dot_nt(a, b):
    return lax.dot_general(a, b, (((1,), (1,)), ((), ())), preferred_element_type=F32)


def levels_of(products, size, level_count):
    out = []
    for level in range(level_count):
        total = None
        for j, product in enumerate(products):
            i = level - j
            if 0 <= i and (i + 1) * size <= product.shape[0]:
                block = product[i * size : (i + 1) * size]
                total = block if total is None else total + block
        out.append(total)
    return out


def combine(leading, rest):
    high, low = leading[0], None
    for part in leading[1:]:
        high, error = two_sum(high, part)
        low = error if low is None else low + error
    tail = None
    for level in reversed(rest):
        tail = level if tail is None else level + tail * (1.0 / 256.0)
    tail = tail * (1.0 / 256.0)
    low = tail if low is None else low + tail
    return two_sum(high, low)


def long_gram(left_ref, left_size, right_ref, right_size, right_count, level_count):
    left_count = left_ref.shape[0] // left_size
    leading, rest = [], None
    for start in range(0, left_ref.shape[1], CHUNK):
        products = []
        for j in range(right_count):
            rows = min(left_count, level_count - j) * left_size
            products.append(
                dot_nt(
                    left_ref[0:rows, start : start + CHUNK],
                    right_ref[j * right_size : (j + 1) * right_size, start : start + CHUNK],
                )
            )
        levels = levels_of(products, left_size, level_count)
        leading.append(levels[0])
        rest = levels[1:] if rest is None else [a + b for a, b in zip(rest, levels[1:])]
    return combine(leading, rest)


def modes_kernel(share, basis_ref, parts_ref, scale_ref, pair_ref, gram_ref):
    size, lanes = basis_ref.shape
    bound = jnp.zeros((size, 1), F32)
    for start in range(0, lanes, CHUNK):
        bound = jnp.maximum(bound, jnp.max(jnp.abs(basis_ref[:, start : start + CHUNK]), axis=1, keepdims=True))
    scale, inverse = power_of_two(bound)
    scale_ref[...] = scale
    for start in range(0, lanes, PIECE):
        block = basis_ref[:, start : start + PIECE]
        for index, part in enumerate(slices_of(block, None, inverse, MODE_SLICES)):
            parts_ref[index * size : (index + 1) * size, start : start + PIECE] = part.astype(BF16)
        rounded = block.astype(BF16)
        pair_ref[0:size, start : start + PIECE] = rounded
        pair_ref[size : 2 * size, start : start + PIECE] = (block - rounded.astype(F32)).astype(BF16)
    high, low = long_gram(parts_ref, size, parts_ref, size, MODE_SLICES, MODE_SLICES)
    factor = scale * (1.0 / 16384.0)
    across = to_row(scale)
    gram_ref[...] = (high * factor * across - jnp.where(eye_mask(size), share, 0.0)) + low * factor * across


def cyclic(size):
    rows, lanes = iota((size, size), 0), iota((size, size), 1)
    return (lanes == rows + 1) | ((rows == size - 1) & (lanes == 0))


def columns_kernel(
    ids_ref, archive_ref, parts, scale_ref, gram_ref, columns_ref, packed_ref, slices
):
    count = ids_ref.shape[0]
    total, lanes = archive_ref.shape
    modes = scale_ref.shape[0]
    starts = range(0, lanes, CHUNK)
    picker = jnp.where(ids_ref[...] == iota((count, total), 1), 1.0, 0.0).astype(BF16)
    bound = jnp.zeros((count, 1), F32)
    for start in range(0, lanes, PIECE):
        block = jnp.dot(picker, archive_ref[:, start : start + PIECE], preferred_element_type=F32)
        columns_ref[:, start : start + PIECE] = block.astype(BF16)
        bound = jnp.maximum(bound, jnp.max(jnp.abs(block), axis=1, keepdims=True))
    scale, inverse = power_of_two(bound)
    for start in range(0, lanes, PIECE):
        block = columns_ref[:, start : start + PIECE].astype(F32)
        for index, part in enumerate(slices_of(block, None, inverse, COLUMN_SLICES)):
            slices[index * count : (index + 1) * count, start : start + PIECE] = part.astype(BF16)

    whole, lead_p, lead_c = None, [], []
    height = MODE_SLICES * modes
    for start in starts:
        right = slices[:, start : start + CHUNK]
        product = dot_nt(jnp.concatenate([parts[:, start : start + CHUNK], right], axis=0), right)
        lead_p.append(product[0:modes, 0:count])
        lead_c.append(product[height : height + count, 0:count])
        whole = product if whole is None else whole + product
    by_slice = [whole[:, j * count : (j + 1) * count] for j in range(COLUMN_SLICES)]
    last = MODE_SLICES + COLUMN_SLICES - 2
    p_high, p_low = combine(lead_p, levels_of([part[0:height] for part in by_slice], modes, last)[1:])
    last = 2 * COLUMN_SLICES - 1
    c_high, c_low = combine(lead_c, levels_of([part[height:] for part in by_slice], count, last)[1:])
    across = to_row(scale)
    factor = scale_ref[...] * (1.0 / 16384.0)
    p_high, p_low = p_high * factor * across, p_low * factor * across
    factor = scale * (1.0 / 16384.0)
    c_high, c_low = c_high * factor * across, c_low * factor * across
    n = count
    gram = gram_ref[...]
    last_block = gram[n:, n:]
    last_diagonal = jnp.sum(jnp.where(eye_mask(n), last_block, 0.0), axis=1, keepdims=True)
    c_low = jnp.where(cyclic(n), last_diagonal, c_low)
    corner = jnp.where(iota((n, n), 0) >= iota((n, n), 1), gram[0:n, 0:n], last_block)
    top = jnp.concatenate([p_high[0:n], p_low[0:n], p_high[n:], p_low[n:]], axis=1)
    low = jnp.concatenate([c_high, c_low, gram[n:, 0:n], corner], axis=1)
    for index in range(packed_ref.shape[0]):
        packed_ref[index, 0:n, :] = top
        packed_ref[index, n:, :] = low


def sum_pairs(parts_ref):
    high = parts_ref[0]
    error = jnp.zeros_like(high)
    for index in range(1, parts_ref.shape[0]):
        high, part = two_sum(high, parts_ref[index])
        error = error + part
    n = high.shape[0] // 2
    rows, lanes = iota(high.shape, 0), iota(high.shape, 1)
    top_takes = (rows < n) & ((lanes // n) % 2 == 1)
    row, lane = rows - n, lanes - n
    special = (lane == row + 1) | ((row == n - 1) & (lane == 0))
    takes = top_takes | ((row >= 0) & (lane >= 0) & (lane < n) & jnp.logical_not(special))
    return jnp.where(takes, high + pltpu.roll(error, n, 1), high)


def sum_kernel(parts_ref, out_ref):
    total = sum_pairs(parts_ref)
    for index in range(out_ref.shape[0]):
        out_ref[index] = total


def high_dot(a, b):
    return jnp.dot(a, b, precision=HIGH, preferred_element_type=F32)


def widen(a):
    return jnp.concatenate([a, jnp.zeros((a.shape[0], 128 - a.shape[1]), F32)], axis=1)


def pieces_of(a):
    high = a.astype(BF16)
    rest = a - high.astype(F32)
    middle = rest.astype(BF16)
    return high, middle, (rest - middle.astype(F32)).astype(BF16)


def wide_dot(left, right):
    a_high, a_middle, a_low = left
    b_high, b_middle, b_low = right
    none = jnp.zeros((128 - b_high.shape[0], 128), BF16)

    def long_dot(across, down):
        down = [block for piece in down for block in (piece, none)]
        return jnp.dot(jnp.concatenate(across, axis=1), jnp.concatenate(down, axis=0), preferred_element_type=F32)

    return long_dot((a_low, a_high, a_middle), (b_high, b_low, b_middle)) + long_dot(
        (a_middle, a_high, a_high), (b_high, b_middle, b_high)
    )


def slice_product(left, right, level_count):
    size = left[0].shape[0]
    stacked = jnp.concatenate(left, axis=0).astype(BF16)
    products = []
    for j, part in enumerate(right):
        rows = (level_count - j) * size
        products.append(jnp.dot(stacked[0:rows], part.astype(BF16), preferred_element_type=F32))
    levels = levels_of(products, size, level_count)
    return combine(levels[0:1], levels[1:])


def triangle(high, low):
    size = high.shape[0]
    rows = iota((size, size), 0)
    for j in range(size - 1):
        row_high, row_low = high[j : j + 1, :], low[j : j + 1, :]
        below = iota((size, 1), 0) > j
        col_high = jnp.where(below, high[:, j : j + 1], 0.0)
        col_low = jnp.where(below, low[:, j : j + 1], 0.0)
        d_high, d_low = row_high[:, j : j + 1], row_low[:, j : j + 1]
        q_high = 1.0 / d_high
        p_high, p_low = two_product(d_high, q_high)
        q_low = q_high * (((1.0 - p_high) - p_low) - d_low * q_high)
        w_high, w_error = two_product(col_high, q_high)
        w_low = w_error + (col_high * q_low + col_low * q_high)
        u_high, u_error = two_product(w_high, row_high)
        u_low = u_error + (w_high * row_low + w_low * row_high)
        s_high, s_error = two_sum(high, -u_high)
        s_low = s_error + (low - u_low)
        high = s_high + s_low
        low = s_low - (high - s_high)
    pivots = jnp.sum(jnp.where(eye_mask(size), high, 0.0), axis=1, keepdims=True)
    return jnp.where(iota((size, size), 1) >= rows, high * lax.rsqrt(pivots), 0.0)


def dense(packed, values, total_rows):
    n = packed.shape[0] // 2
    m = 2 * n
    width = m + n
    square_scale = 1.0 / total_rows
    scale = math.sqrt(square_scale)

    def block(row, lane):
        return packed[row * n : (row + 1) * n, lane * n : (lane + 1) * n]

    p_high = jnp.concatenate([block(0, 0), block(0, 2)], axis=0)
    p_low = jnp.concatenate([block(0, 1), block(0, 3)], axis=0)
    p_high, p_low = two_sum(p_high, p_low)
    stored, corner, side = block(1, 1), block(1, 3), block(1, 2)
    special = cyclic(n)
    last_diagonal = jnp.sum(jnp.where(special, stored, 0.0), axis=1, keepdims=True)
    c_high, c_low = two_sum(block(1, 0), jnp.where(special, stored.T, stored))
    rows, lanes = iota((n, n), 0), iota((n, n), 1)
    turned_corner = corner.T
    first_block = jnp.where(rows >= lanes, corner, turned_corner)
    last_block = jnp.where(rows > lanes, turned_corner, jnp.where(rows < lanes, corner, last_diagonal))
    excess = jnp.concatenate(
        [jnp.concatenate([first_block, side.T], axis=1), jnp.concatenate([side, last_block], axis=1)], axis=0
    )
    eye_m = jnp.where(eye_mask(m), 1.0, 0.0)
    t_high, t_low = two_sum(eye_m, -excess)

    t_scale, t_inverse = power_of_two(jnp.max(jnp.max(jnp.abs(t_high), axis=1, keepdims=True), axis=0, keepdims=True))
    p_scale, p_inverse = power_of_two(jnp.max(jnp.abs(p_high), axis=0, keepdims=True))
    p_slices = slices_of(p_high, p_low, p_inverse, DENSE_SLICES)
    h_high, h_low = slice_product(slices_of(t_high, t_low, t_inverse, DENSE_SLICES), p_slices, DENSE_SLICES)
    h_scale, h_inverse = power_of_two(jnp.max(jnp.abs(h_high), axis=0, keepdims=True))
    pt_slices = [part.T for part in p_slices]
    q_high, q_low = slice_product(pt_slices, slices_of(h_high, h_low, h_inverse, DENSE_SLICES), DENSE_SLICES)
    factor = to_column(p_scale) * (1.0 / 16384.0)
    across = h_scale * (p_scale * (t_scale * (1.0 / 16384.0)))
    q_high, q_low = q_high * factor * across, q_low * factor * across
    r_high, r_error = two_sum(c_high, -q_high)
    one_high, one_low = two_sum(r_high, r_error + (c_low - q_low))

    eye_n = eye_mask(n)
    own = jnp.sum(jnp.where(eye_n, one_high, 0.0), axis=0, keepdims=True)
    energy = jnp.sum(jnp.where(eye_n, c_high, 0.0), axis=0, keepdims=True)
    novelty = own / energy

    values_column = to_column(values)
    projection = p_high * scale
    gram = one_high * square_scale
    turned = projection.T
    mixed = projection * values_column
    kernel_top = jnp.concatenate([eye_m * (values_column * values_column), mixed], axis=1)
    kernel_low = jnp.concatenate([mixed.T, high_dot(turned, projection) + gram], axis=1)
    inner = jnp.concatenate([kernel_top, kernel_low], axis=0)
    eye_w = jnp.where(eye_mask(width), 1.0, 0.0)
    total = jnp.sum(jnp.sum(inner * eye_w, axis=1, keepdims=True), axis=0, keepdims=True)
    shifted = widen((inner - (total / width) * eye_w) / total)
    slope = eye = widen(eye_w)
    origin = -1.0 / width
    for _ in range(NEWTON):
        pieces = pieces_of(shifted)
        squared = wide_dot(pieces, pieces)
        divided = (origin * origin) * eye + origin * shifted + squared
        slope = 1.5 * slope - 0.5 * wide_dot(pieces_of(slope), pieces_of(divided))
        shifted = 1.5 * shifted - 0.5 * wide_dot(pieces, pieces_of(squared))
        origin = 1.5 * origin - 0.5 * origin * origin * origin
    blend = 0.5 * (eye_w + shifted[:, 0:width])
    slope = slope[:, 0:width] * (0.5 / total)

    upper = triangle(one_high, one_low) * scale
    core = jnp.concatenate(
        [
            jnp.concatenate([eye_m * values_column, projection], axis=1),
            jnp.concatenate([jnp.zeros((n, m), F32), upper], axis=1),
        ],
        axis=0,
    )
    half = high_dot(core, slope)
    projector = (0.5 * (1.0 + origin)) * eye_w + lax.dot_general(
        half, core, (((1,), (1,)), ((), ())), precision=HIGH, preferred_element_type=F32
    )
    weights = jnp.concatenate([blend[:, 0:m] * (values * math.sqrt(total_rows)), blend[:, m:]], axis=1)
    return weights, projector, novelty


def finish_kernel(
    total_rows,
    packed_ref,
    values_ref,
    pair,
    columns,
    filtered_hbm,
    projector_ref,
    novelty_ref,
    filtered,
    left_sem,
):
    modes = values_ref.shape[1]
    lanes = pair.shape[1]
    weights, projector, novelty = dense(sum_pairs(packed_ref), values_ref[...], total_rows)
    rounded = weights.astype(BF16)
    rest = (weights - rounded.astype(F32)).astype(BF16)
    left = jnp.concatenate(
        [rounded[:, 0:modes], rounded[:, 0:modes], rest[:, 0:modes], rounded[:, modes:], rest[:, modes:]], axis=1
    )
    stores = []
    for start in range(0, lanes, PIECE):
        where = slice(start, start + PIECE)
        first, second, third = pair[0:modes, where], pair[modes:, where], columns[:, where]
        right = jnp.concatenate([first, second, first, third, third], axis=0)
        filtered[:, where] = jnp.dot(left, right, preferred_element_type=F32)
        store = pltpu.make_async_copy(
            filtered.at[:, pl.ds(start, PIECE)], filtered_hbm.at[:, pl.ds(start, PIECE)], left_sem.at[len(stores)]
        )
        store.start()
        stores.append(store)
    projector_ref[...] = projector
    novelty_ref[...] = novelty
    for store in stores:
        store.wait()


def vmem(count):
    return [pl.BlockSpec(memory_space=pltpu.VMEM)] * count


def shape(dims, dtype=F32):
    return jax.ShapeDtypeStruct(dims, dtype)


def kept(dims, dtype=F32):
    return shape(dims, dtype) if INTERPRET else pltpu.VMEM(dims, dtype)


def params():
    return pltpu.CompilerParams(vmem_limit_bytes=24 * 1024 * 1024)


def prepare(basis, share):
    modes, lanes = basis.shape
    return pl.pallas_call(
        functools.partial(modes_kernel, share),
        out_shape=(
            kept((MODE_SLICES * modes, lanes), BF16),
            kept((modes, 1)),
            kept((2 * modes, lanes), BF16),
            kept((modes, modes)),
        ),
        in_specs=vmem(1),
        out_specs=tuple(vmem(4)),
        interpret=INTERPRET,
        compiler_params=params(),
        name="modes",
    )(basis)


def gather(ids, everything, parts, scale, gram, copies):
    count, lanes = ids.shape[0], everything.shape[1]
    return pl.pallas_call(
        columns_kernel,
        out_shape=(kept((count, lanes), BF16), kept((copies, 2 * count, 128))),
        in_specs=vmem(5),
        out_specs=tuple(vmem(2)),
        scratch_shapes=[
            pltpu.VMEM((COLUMN_SLICES * count, lanes), BF16),
        ],
        interpret=INTERPRET,
        compiler_params=params(),
        name="columns",
    )(ids, everything, parts, scale, gram)


def add_up(parts, copies):
    return pl.pallas_call(
        sum_kernel,
        out_shape=kept((copies,) + parts.shape[1:]),
        in_specs=vmem(1),
        out_specs=vmem(1)[0],
        interpret=INTERPRET,
        compiler_params=params(),
        name="add",
    )(parts)


def finish(total_rows, packed, values, pair, columns):
    modes, count, lanes = values.shape[1], columns.shape[0], columns.shape[1]
    width = modes + count
    anywhere = pl.BlockSpec(memory_space=pl.ANY)
    return pl.pallas_call(
        functools.partial(finish_kernel, total_rows),
        out_shape=(shape((width, lanes)), shape((width, width)), shape((1, count))),
        in_specs=vmem(4),
        out_specs=(anywhere,) + tuple(vmem(2)),
        scratch_shapes=[
            pltpu.VMEM((width, lanes), F32),
            pltpu.SemaphoreType.DMA((lanes // PIECE,)),
        ],
        interpret=INTERPRET,
        compiler_params=params(),
        name="finish",
    )(packed, values, pair, columns)


def exchange(copies, axes):
    return near(lax.all_to_all(copies, axes, 0, 0, tiled=True))


def near(array):
    return pltpu.with_memory_space_constraint(array, pltpu.VMEM)


def per_device(basis, values, archive, window_ids):
    devices = 1
    for name in ALL:
        devices *= lax.axis_size(name)
    total_rows = basis.shape[1] * devices
    everything = near(lax.all_to_all(archive, ("x", "c"), split_axis=1, concat_axis=0, tiled=True))
    parts, scale, pair, gram = prepare(basis, 1.0 / devices)
    columns, packed = gather(near(window_ids[:, None]), everything, parts, scale, gram, lax.axis_size("y"))
    packed = add_up(exchange(packed, ("y",)), lax.axis_size("z"))
    packed = add_up(exchange(packed, ("z",)), lax.axis_size("x") * lax.axis_size("c"))
    packed = exchange(packed, ("x", "c"))
    filtered, projector, novelty = finish(total_rows, packed, near(values[None, :]), pair, columns)
    return (filtered, projector, novelty.reshape(-1))


def solution(mesh):
    fine = Mesh(mesh.devices.reshape(8, 8, 4, 2), ALL)
    placed = (P(None, ALL), P(), P(("x", "c"), ("y", "z")), P())
    return jax.shard_map(
        per_device,
        mesh=fine,
        in_specs=placed,
        out_specs=(P(None, ALL), P(), P()),
        check_vma=False,
    )
```

```python
import functools
import math

import jax
import jax.numpy as jnp
from jax import lax
from jax.experimental import pallas as pl
from jax.experimental.pallas import tpu as pltpu
from jax.sharding import Mesh, PartitionSpec as P

NEWTON = 10
HIGH = lax.Precision.HIGHEST
ALL = ("y", "z", "x", "c")
F32 = jnp.float32
BF16 = jnp.bfloat16
MODE_SLICES = 4
COLUMN_SLICES = 3
DENSE_SLICES = 5
CHUNK = 1024
PIECE = 512
INTERPRET = False


def iota(shape, axis):
    return lax.broadcasted_iota(jnp.int32, shape, axis)


def eye_mask(size):
    return iota((size, size), 0) == iota((size, size), 1)


def to_column(row):
    size = row.shape[1]
    return jnp.sum(jnp.where(eye_mask(size), row, 0.0), axis=1, keepdims=True)


def to_row(column):
    size = column.shape[0]
    return jnp.sum(jnp.where(eye_mask(size), column, 0.0), axis=0, keepdims=True)


def two_sum(a, b):
    total = a + b
    part = total - a
    return total, (a - (total - part)) + (b - part)


def split(a):
    scaled = a * 4097.0
    high = scaled - (scaled - a)
    return high, a - high


def two_product(a, b):
    product = a * b
    a_high, a_low = split(a)
    b_high, b_low = split(b)
    error = ((a_high * b_high - product) + a_high * b_low + a_low * b_high) + a_low * b_low
    return product, error


def power_of_two(bound):
    rest = bound
    scale = jnp.full_like(bound, 2.0)
    inverse = jnp.full_like(bound, 0.5)
    for step in (64, 32, 16, 8, 4, 2, 1):
        up, down = float(2.0**step), float(2.0**-step)
        large = rest >= up
        rest = jnp.where(large, rest * down, rest)
        scale = jnp.where(large, scale * up, scale)
        inverse = jnp.where(large, inverse * down, inverse)
    for step in (32, 16, 8, 4, 2, 1):
        up, down = float(2.0**step), float(2.0**-step)
        small = rest < 2.0 * down
        rest = jnp.where(small, rest * up, rest)
        scale = jnp.where(small, scale * down, scale)
        inverse = jnp.where(small, inverse * up, inverse)
    return scale, inverse


def slices_of(high, low, inverse, count):
    rest = high * (inverse * 128.0)
    out = []
    for index in range(count):
        if index == 2 and low is not None:
            rest = rest + low * (inverse * (128.0 * 65536.0))
        whole = jnp.round(rest)
        out.append(whole)
        if index + 1 < count:
            rest = (rest - whole) * 256.0
    return out


def dot_nt(a, b):
    return lax.dot_general(a, b, (((1,), (1,)), ((), ())), preferred_element_type=F32)


def levels_of(products, size, level_count):
    out = []
    for level in range(level_count):
        total = None
        for j, product in enumerate(products):
            i = level - j
            if 0 <= i and (i + 1) * size <= product.shape[0]:
                block = product[i * size : (i + 1) * size]
                total = block if total is None else total + block
        out.append(total)
    return out


def combine(leading, rest):
    high, low = leading[0], None
    for part in leading[1:]:
        high, error = two_sum(high, part)
        low = error if low is None else low + error
    tail = None
    for level in reversed(rest):
        tail = level if tail is None else level + tail * (1.0 / 256.0)
    tail = tail * (1.0 / 256.0)
    low = tail if low is None else low + tail
    return two_sum(high, low)


def long_gram(left_ref, left_size, right_ref, right_size, right_count, level_count):
    left_count = left_ref.shape[0] // left_size
    leading, rest = [], None
    for start in range(0, left_ref.shape[1], CHUNK):
        products = []
        for j in range(right_count):
            rows = min(left_count, level_count - j) * left_size
            products.append(
                dot_nt(
                    left_ref[0:rows, start : start + CHUNK],
                    right_ref[j * right_size : (j + 1) * right_size, start : start + CHUNK],
                )
            )
        levels = levels_of(products, left_size, level_count)
        leading.append(levels[0])
        rest = levels[1:] if rest is None else [a + b for a, b in zip(rest, levels[1:])]
    return combine(leading, rest)


def modes_kernel(share, basis_ref, parts_ref, scale_ref, pair_ref, gram_ref):
    size, lanes = basis_ref.shape
    bound = jnp.zeros((size, 1), F32)
    for start in range(0, lanes, CHUNK):
        bound = jnp.maximum(bound, jnp.max(jnp.abs(basis_ref[:, start : start + CHUNK]), axis=1, keepdims=True))
    scale, inverse = power_of_two(bound)
    scale_ref[...] = scale
    for start in range(0, lanes, PIECE):
        block = basis_ref[:, start : start + PIECE]
        for index, part in enumerate(slices_of(block, None, inverse, MODE_SLICES)):
            parts_ref[index * size : (index + 1) * size, start : start + PIECE] = part.astype(BF16)
        rounded = block.astype(BF16)
        pair_ref[0:size, start : start + PIECE] = rounded
        pair_ref[size : 2 * size, start : start + PIECE] = (block - rounded.astype(F32)).astype(BF16)
    high, low = long_gram(parts_ref, size, parts_ref, size, MODE_SLICES, MODE_SLICES)
    factor = scale * (1.0 / 16384.0)
    across = to_row(scale)
    gram_ref[...] = (high * factor * across - jnp.where(eye_mask(size), share, 0.0)) + low * factor * across


def cyclic(size):
    rows, lanes = iota((size, size), 0), iota((size, size), 1)
    return (lanes == rows + 1) | ((rows == size - 1) & (lanes == 0))


def columns_kernel(
    ids_ref, archive_ref, parts, scale_ref, gram_ref, columns_ref, packed_ref, slices
):
    count = ids_ref.shape[0]
    total, lanes = archive_ref.shape
    modes = scale_ref.shape[0]
    starts = range(0, lanes, CHUNK)
    picker = jnp.where(ids_ref[...] == iota((count, total), 1), 1.0, 0.0).astype(BF16)
    bound = jnp.zeros((count, 1), F32)
    for start in range(0, lanes, PIECE):
        block = jnp.dot(picker, archive_ref[:, start : start + PIECE], preferred_element_type=F32)
        columns_ref[:, start : start + PIECE] = block.astype(BF16)
        bound = jnp.maximum(bound, jnp.max(jnp.abs(block), axis=1, keepdims=True))
    scale, inverse = power_of_two(bound)
    for start in range(0, lanes, PIECE):
        block = columns_ref[:, start : start + PIECE].astype(F32)
        for index, part in enumerate(slices_of(block, None, inverse, COLUMN_SLICES)):
            slices[index * count : (index + 1) * count, start : start + PIECE] = part.astype(BF16)

    whole, lead_p, lead_c = None, [], []
    height = MODE_SLICES * modes
    for start in starts:
        right = slices[:, start : start + CHUNK]
        product = dot_nt(jnp.concatenate([parts[:, start : start + CHUNK], right], axis=0), right)
        lead_p.append(product[0:modes, 0:count])
        lead_c.append(product[height : height + count, 0:count])
        whole = product if whole is None else whole + product
    by_slice = [whole[:, j * count : (j + 1) * count] for j in range(COLUMN_SLICES)]
    last = MODE_SLICES + COLUMN_SLICES - 2
    p_high, p_low = combine(lead_p, levels_of([part[0:height] for part in by_slice], modes, last)[1:])
    last = 2 * COLUMN_SLICES - 1
    c_high, c_low = combine(lead_c, levels_of([part[height:] for part in by_slice], count, last)[1:])
    across = to_row(scale)
    factor = scale_ref[...] * (1.0 / 16384.0)
    p_high, p_low = p_high * factor * across, p_low * factor * across
    factor = scale * (1.0 / 16384.0)
    c_high, c_low = c_high * factor * across, c_low * factor * across
    n = count
    gram = gram_ref[...]
    last_block = gram[n:, n:]
    last_diagonal = jnp.sum(jnp.where(eye_mask(n), last_block, 0.0), axis=1, keepdims=True)
    c_low = jnp.where(cyclic(n), last_diagonal, c_low)
    corner = jnp.where(iota((n, n), 0) >= iota((n, n), 1), gram[0:n, 0:n], last_block)
    top = jnp.concatenate([p_high[0:n], p_low[0:n], p_high[n:], p_low[n:]], axis=1)
    low = jnp.concatenate([c_high, c_low, gram[n:, 0:n], corner], axis=1)
    for index in range(packed_ref.shape[0]):
        packed_ref[index, 0:n, :] = top
        packed_ref[index, n:, :] = low


def sum_pairs(load, count, place, n):
    high = load(0)
    error = jnp.zeros_like(high)
    for index in range(1, count):
        high, part = two_sum(high, load(index))
        error = error + part
    rows, lanes = iota(high.shape, 0), iota(high.shape, 1)
    top_takes = (lanes // n) % 2 == 1
    lane = lanes - n
    special = (lane == rows + 1) | ((rows == n - 1) & (lane == 0))
    low_takes = (lane >= 0) & (lane < n) & jnp.logical_not(special)
    takes = jnp.where(place == 0, jnp.where(top_takes, 1.0, 0.0), jnp.where(low_takes, 1.0, 0.0))
    return high + takes * pltpu.roll(error, n, 1)


def half_kernel(place_ref, both_ref, out_ref):
    copies, rows, _ = out_ref.shape
    start = pl.multiple_of(place_ref[0] * rows, 8)
    total = sum_pairs(lambda index: both_ref[index, pl.ds(start, rows), :], both_ref.shape[0], place_ref[0], rows)
    for index in range(copies):
        out_ref[index] = total


def sum_kernel(place_ref, parts_ref, out_ref):
    rows = parts_ref.shape[1]
    total = sum_pairs(lambda index: parts_ref[index], parts_ref.shape[0], place_ref[0], rows)
    for index in range(out_ref.shape[0]):
        out_ref[index] = total


def high_dot(a, b):
    return jnp.dot(a, b, precision=HIGH, preferred_element_type=F32)


def widen(a):
    return jnp.concatenate([a, jnp.zeros((a.shape[0], 128 - a.shape[1]), F32)], axis=1)


def pieces_of(a):
    high = a.astype(BF16)
    return high, (a - high.astype(F32)).astype(BF16)


def wide_dot(left, right):
    a_high, a_low = left
    b_high, b_low = right
    none = jnp.zeros((128 - b_high.shape[0], 128), BF16)
    down = jnp.concatenate([b_high, none, b_low, none, b_high, none], axis=0)
    return jnp.dot(jnp.concatenate([a_low, a_high, a_high], axis=1), down, preferred_element_type=F32)


def slice_product(left, right, level_count):
    size = left[0].shape[0]
    stacked = jnp.concatenate(left, axis=0).astype(BF16)
    products = []
    for j, part in enumerate(right):
        rows = (level_count - j) * size
        products.append(jnp.dot(stacked[0:rows], part.astype(BF16), preferred_element_type=F32))
    levels = levels_of(products, size, level_count)
    return combine(levels[0:1], levels[1:])


def triangle(high, low):
    size = high.shape[0]
    rows = iota((size, size), 0)
    for j in range(size - 1):
        row_high, row_low = high[j : j + 1, :], low[j : j + 1, :]
        below = iota((size, 1), 0) > j
        col_high = jnp.where(below, high[:, j : j + 1], 0.0)
        col_low = jnp.where(below, low[:, j : j + 1], 0.0)
        d_high, d_low = row_high[:, j : j + 1], row_low[:, j : j + 1]
        q_high = 1.0 / d_high
        p_high, p_low = two_product(d_high, q_high)
        q_low = q_high * (((1.0 - p_high) - p_low) - d_low * q_high)
        w_high, w_error = two_product(col_high, q_high)
        w_low = w_error + (col_high * q_low + col_low * q_high)
        u_high, u_error = two_product(w_high, row_high)
        u_low = u_error + (w_high * row_low + w_low * row_high)
        s_high, s_error = two_sum(high, -u_high)
        s_low = s_error + (low - u_low)
        high = s_high + s_low
        low = s_low - (high - s_high)
    pivots = jnp.sum(jnp.where(eye_mask(size), high, 0.0), axis=1, keepdims=True)
    return jnp.where(iota((size, size), 1) >= rows, high * lax.rsqrt(pivots), 0.0)


def dense(packed, values, total_rows):
    n = packed.shape[0] // 2
    m = 2 * n
    width = m + n
    square_scale = 1.0 / total_rows
    scale = math.sqrt(square_scale)

    def block(row, lane):
        return packed[row * n : (row + 1) * n, lane * n : (lane + 1) * n]

    p_high = jnp.concatenate([block(0, 0), block(0, 2)], axis=0)
    p_low = jnp.concatenate([block(0, 1), block(0, 3)], axis=0)
    p_high, p_low = two_sum(p_high, p_low)
    stored, corner, side = block(1, 1), block(1, 3), block(1, 2)
    special = cyclic(n)
    last_diagonal = jnp.sum(jnp.where(special, stored, 0.0), axis=1, keepdims=True)
    c_high, c_low = two_sum(block(1, 0), jnp.where(special, stored.T, stored))
    rows, lanes = iota((n, n), 0), iota((n, n), 1)
    turned_corner = corner.T
    first_block = jnp.where(rows >= lanes, corner, turned_corner)
    last_block = jnp.where(rows > lanes, turned_corner, jnp.where(rows < lanes, corner, last_diagonal))
    excess = jnp.concatenate(
        [jnp.concatenate([first_block, side.T], axis=1), jnp.concatenate([side, last_block], axis=1)], axis=0
    )
    eye_m = jnp.where(eye_mask(m), 1.0, 0.0)
    t_high, t_low = two_sum(eye_m, -excess)

    t_scale, t_inverse = power_of_two(jnp.max(jnp.max(jnp.abs(t_high), axis=1, keepdims=True), axis=0, keepdims=True))
    p_scale, p_inverse = power_of_two(jnp.max(jnp.abs(p_high), axis=0, keepdims=True))
    p_slices = slices_of(p_high, p_low, p_inverse, DENSE_SLICES)
    h_high, h_low = slice_product(slices_of(t_high, t_low, t_inverse, DENSE_SLICES), p_slices, DENSE_SLICES)
    h_scale, h_inverse = power_of_two(jnp.max(jnp.abs(h_high), axis=0, keepdims=True))
    pt_slices = [part.T for part in p_slices]
    q_high, q_low = slice_product(pt_slices, slices_of(h_high, h_low, h_inverse, DENSE_SLICES), DENSE_SLICES)
    factor = to_column(p_scale) * (1.0 / 16384.0)
    across = h_scale * (p_scale * (t_scale * (1.0 / 16384.0)))
    q_high, q_low = q_high * factor * across, q_low * factor * across
    r_high, r_error = two_sum(c_high, -q_high)
    one_high, one_low = two_sum(r_high, r_error + (c_low - q_low))

    eye_n = eye_mask(n)
    own = jnp.sum(jnp.where(eye_n, one_high, 0.0), axis=0, keepdims=True)
    energy = jnp.sum(jnp.where(eye_n, c_high, 0.0), axis=0, keepdims=True)
    novelty = own / energy

    values_column = to_column(values)
    projection = p_high * scale
    turned = projection.T
    mixed = projection * values_column
    kernel_top = jnp.concatenate([eye_m * (values_column * values_column), mixed], axis=1)
    gram = one_high * square_scale
    kernel_low = jnp.concatenate([mixed.T, high_dot(turned, projection) + gram], axis=1)
    inner = jnp.concatenate([kernel_top, kernel_low], axis=0)
    eye_w = jnp.where(eye_mask(width), 1.0, 0.0)
    total = jnp.sum(jnp.sum(inner * eye_w, axis=1, keepdims=True), axis=0, keepdims=True)
    shifted = widen((inner - (total / width) * eye_w) / total)
    slope = eye = widen(eye_w)
    origin = -1.0 / width
    for _ in range(NEWTON):
        pieces = pieces_of(shifted)
        squared = wide_dot(pieces, pieces)
        divided = (origin * origin) * eye + origin * shifted + squared
        slope = 1.5 * slope - 0.5 * wide_dot(pieces_of(slope), pieces_of(divided))
        shifted = 1.5 * shifted - 0.5 * wide_dot(pieces, pieces_of(squared))
        origin = 1.5 * origin - 0.5 * origin * origin * origin
    blend = 0.5 * (eye_w + shifted[:, 0:width])
    slope = slope[:, 0:width] * (0.5 / total)

    upper = triangle(one_high, one_low) * scale
    core = jnp.concatenate(
        [
            jnp.concatenate([eye_m * values_column, projection], axis=1),
            jnp.concatenate([jnp.zeros((n, m), F32), upper], axis=1),
        ],
        axis=0,
    )
    half = high_dot(core, slope)
    projector = (0.5 * (1.0 + origin)) * eye_w + lax.dot_general(
        half, core, (((1,), (1,)), ((), ())), precision=HIGH, preferred_element_type=F32
    )
    weights = jnp.concatenate([blend[:, 0:m] * (values * math.sqrt(total_rows)), blend[:, m:]], axis=1)
    return weights, projector, novelty


def finish_kernel(
    total_rows,
    packed_ref,
    values_ref,
    pair,
    columns,
    filtered_hbm,
    projector_ref,
    novelty_ref,
    filtered,
    left_sem,
):
    modes = values_ref.shape[1]
    lanes = pair.shape[1]
    weights, projector, novelty = dense(packed_ref[0], values_ref[...], total_rows)
    rounded = weights.astype(BF16)
    rest = (weights - rounded.astype(F32)).astype(BF16)
    left = jnp.concatenate(
        [rounded[:, 0:modes], rounded[:, 0:modes], rest[:, 0:modes], rounded[:, modes:], rest[:, modes:]], axis=1
    )
    stores = []
    for start in range(0, lanes, PIECE):
        where = slice(start, start + PIECE)
        first, second, third = pair[0:modes, where], pair[modes:, where], columns[:, where]
        right = jnp.concatenate([first, second, first, third, third], axis=0)
        filtered[:, where] = jnp.dot(left, right, preferred_element_type=F32)
        store = pltpu.make_async_copy(
            filtered.at[:, pl.ds(start, PIECE)], filtered_hbm.at[:, pl.ds(start, PIECE)], left_sem.at[len(stores)]
        )
        store.start()
        stores.append(store)
    projector_ref[...] = projector
    novelty_ref[...] = novelty
    for store in stores:
        store.wait()


def vmem(count):
    return [pl.BlockSpec(memory_space=pltpu.VMEM)] * count


def shape(dims, dtype=F32):
    return jax.ShapeDtypeStruct(dims, dtype)


def kept(dims, dtype=F32):
    return shape(dims, dtype) if INTERPRET else pltpu.VMEM(dims, dtype)


def params():
    return pltpu.CompilerParams(vmem_limit_bytes=24 * 1024 * 1024)


def prepare(basis, share):
    modes, lanes = basis.shape
    return pl.pallas_call(
        functools.partial(modes_kernel, share),
        out_shape=(
            kept((MODE_SLICES * modes, lanes), BF16),
            kept((modes, 1)),
            kept((2 * modes, lanes), BF16),
            kept((modes, modes)),
        ),
        in_specs=vmem(1),
        out_specs=tuple(vmem(4)),
        interpret=INTERPRET,
        compiler_params=params(),
        name="modes",
    )(basis)


def gather(ids, everything, parts, scale, gram, copies):
    count, lanes = ids.shape[0], everything.shape[1]
    return pl.pallas_call(
        columns_kernel,
        out_shape=(kept((count, lanes), BF16), kept((copies, 2 * count, 128))),
        in_specs=vmem(5),
        out_specs=tuple(vmem(2)),
        scratch_shapes=[
            pltpu.VMEM((COLUMN_SLICES * count, lanes), BF16),
        ],
        interpret=INTERPRET,
        compiler_params=params(),
        name="columns",
    )(ids, everything, parts, scale, gram)


def add_up(place, parts, copies):
    return pl.pallas_call(
        sum_kernel,
        out_shape=kept((copies,) + parts.shape[1:]),
        in_specs=[pl.BlockSpec(memory_space=pltpu.SMEM)] + vmem(1),
        out_specs=vmem(1)[0],
        interpret=INTERPRET,
        compiler_params=params(),
        name="add",
    )(place, parts)


def take_half(place, both, copies):
    return pl.pallas_call(
        half_kernel,
        out_shape=kept((copies, both.shape[1] // 2, 128)),
        in_specs=[pl.BlockSpec(memory_space=pltpu.SMEM)] + vmem(1),
        out_specs=vmem(1)[0],
        interpret=INTERPRET,
        compiler_params=params(),
        name="half",
    )(place, both)


def finish(total_rows, packed, values, pair, columns):
    modes, count, lanes = values.shape[1], columns.shape[0], columns.shape[1]
    width = modes + count
    anywhere = pl.BlockSpec(memory_space=pl.ANY)
    return pl.pallas_call(
        functools.partial(finish_kernel, total_rows),
        out_shape=(shape((width, lanes)), shape((width, width)), shape((1, count))),
        in_specs=vmem(4),
        out_specs=(anywhere,) + tuple(vmem(2)),
        scratch_shapes=[
            pltpu.VMEM((width, lanes), F32),
            pltpu.SemaphoreType.DMA((lanes // PIECE,)),
        ],
        interpret=INTERPRET,
        compiler_params=params(),
        name="finish",
    )(packed, values, pair, columns)


def exchange(copies, axes):
    return near(lax.all_to_all(copies, axes, 0, 0, tiled=True))


def near(array):
    return pltpu.with_memory_space_constraint(array, pltpu.VMEM)


def per_device(basis, values, archive, window_ids):
    devices = 1
    for name in ALL:
        devices *= lax.axis_size(name)
    total_rows = basis.shape[1] * devices
    everything = near(lax.all_to_all(archive, ("x", "c"), split_axis=1, concat_axis=0, tiled=True))
    parts, scale, pair, gram = prepare(basis, 1.0 / devices)
    columns, packed = gather(near(window_ids[:, None]), everything, parts, scale, gram, 1)
    place = lax.axis_index("c").astype(jnp.int32)[None]
    both = near(lax.all_gather(packed, "c", axis=0, tiled=True))
    packed = take_half(place, both, lax.axis_size("y"))
    packed = add_up(place, exchange(packed, ("y",)), lax.axis_size("z"))
    packed = add_up(place, exchange(packed, ("z",)), lax.axis_size("x"))
    packed = add_up(place, exchange(packed, ("x",)), 1)
    packed = near(lax.all_gather(packed, "c", axis=1, tiled=True))
    filtered, projector, novelty = finish(total_rows, packed, near(values[None, :]), pair, columns)
    return (filtered, projector, novelty.reshape(-1))


def solution(mesh):
    fine = Mesh(mesh.devices.reshape(8, 8, 4, 2), ALL)
    placed = (P(None, ALL), P(), P(("x", "c"), ("y", "z")), P())
    return jax.shard_map(
        per_device,
        mesh=fine,
        in_specs=placed,
        out_specs=(P(None, ALL), P(), P()),
        check_vma=False,
    )
```

```python
import functools
import math

import jax
import jax.numpy as jnp
from jax import lax
from jax.experimental import pallas as pl
from jax.experimental.pallas import tpu as pltpu
from jax.sharding import Mesh, PartitionSpec as P

NEWTON = 10
HIGH = lax.Precision.HIGHEST
ALL = ("y", "z", "x", "c")
F32 = jnp.float32
BF16 = jnp.bfloat16
MODE_SLICES = 4
COLUMN_SLICES = 3
DENSE_SLICES = 5
CHUNK = 1024
PIECE = 512
INTERPRET = False


def iota(shape, axis):
    return lax.broadcasted_iota(jnp.int32, shape, axis)


def eye_mask(size):
    return iota((size, size), 0) == iota((size, size), 1)


def to_column(row):
    size = row.shape[1]
    return jnp.sum(jnp.where(eye_mask(size), row, 0.0), axis=1, keepdims=True)


def to_row(column):
    size = column.shape[0]
    return jnp.sum(jnp.where(eye_mask(size), column, 0.0), axis=0, keepdims=True)


def two_sum(a, b):
    total = a + b
    part = total - a
    return total, (a - (total - part)) + (b - part)


def split(a):
    scaled = a * 4097.0
    high = scaled - (scaled - a)
    return high, a - high


def two_product(a, b):
    product = a * b
    a_high, a_low = split(a)
    b_high, b_low = split(b)
    error = ((a_high * b_high - product) + a_high * b_low + a_low * b_high) + a_low * b_low
    return product, error


def power_of_two(bound):
    rest = bound
    scale = jnp.full_like(bound, 2.0)
    inverse = jnp.full_like(bound, 0.5)
    for step in (64, 32, 16, 8, 4, 2, 1):
        up, down = float(2.0**step), float(2.0**-step)
        large = rest >= up
        rest = jnp.where(large, rest * down, rest)
        scale = jnp.where(large, scale * up, scale)
        inverse = jnp.where(large, inverse * down, inverse)
    for step in (32, 16, 8, 4, 2, 1):
        up, down = float(2.0**step), float(2.0**-step)
        small = rest < 2.0 * down
        rest = jnp.where(small, rest * up, rest)
        scale = jnp.where(small, scale * down, scale)
        inverse = jnp.where(small, inverse * up, inverse)
    return scale, inverse


def slices_of(high, low, inverse, count):
    rest = high * (inverse * 128.0)
    out = []
    for index in range(count):
        if index == 2 and low is not None:
            rest = rest + low * (inverse * (128.0 * 65536.0))
        whole = jnp.round(rest)
        out.append(whole)
        if index + 1 < count:
            rest = (rest - whole) * 256.0
    return out


def dot_nt(a, b):
    return lax.dot_general(a, b, (((1,), (1,)), ((), ())), preferred_element_type=F32)


def levels_of(products, size, level_count):
    out = []
    for level in range(level_count):
        total = None
        for j, product in enumerate(products):
            i = level - j
            if 0 <= i and (i + 1) * size <= product.shape[0]:
                block = product[i * size : (i + 1) * size]
                total = block if total is None else total + block
        out.append(total)
    return out


def combine(leading, rest):
    high, low = leading[0], None
    for part in leading[1:]:
        high, error = two_sum(high, part)
        low = error if low is None else low + error
    tail = None
    for level in reversed(rest):
        tail = level if tail is None else level + tail * (1.0 / 256.0)
    tail = tail * (1.0 / 256.0)
    low = tail if low is None else low + tail
    return two_sum(high, low)


def long_gram(left_ref, left_size, right_ref, right_size, right_count, level_count):
    left_count = left_ref.shape[0] // left_size
    leading, rest = [], None
    for start in range(0, left_ref.shape[1], CHUNK):
        products = []
        for j in range(right_count):
            rows = min(left_count, level_count - j) * left_size
            products.append(
                dot_nt(
                    left_ref[0:rows, start : start + CHUNK],
                    right_ref[j * right_size : (j + 1) * right_size, start : start + CHUNK],
                )
            )
        levels = levels_of(products, left_size, level_count)
        leading.append(levels[0])
        rest = levels[1:] if rest is None else [a + b for a, b in zip(rest, levels[1:])]
    return combine(leading, rest)


def modes_kernel(share, basis_ref, parts_ref, scale_ref, pair_ref, gram_ref):
    size, lanes = basis_ref.shape
    bound = jnp.zeros((size, 1), F32)
    for start in range(0, lanes, CHUNK):
        bound = jnp.maximum(bound, jnp.max(jnp.abs(basis_ref[:, start : start + CHUNK]), axis=1, keepdims=True))
    scale, inverse = power_of_two(bound)
    scale_ref[...] = scale
    for start in range(0, lanes, PIECE):
        block = basis_ref[:, start : start + PIECE]
        for index, part in enumerate(slices_of(block, None, inverse, MODE_SLICES)):
            parts_ref[index * size : (index + 1) * size, start : start + PIECE] = part.astype(BF16)
        rounded = block.astype(BF16)
        pair_ref[0:size, start : start + PIECE] = rounded
        pair_ref[size : 2 * size, start : start + PIECE] = (block - rounded.astype(F32)).astype(BF16)
    high, low = long_gram(parts_ref, size, parts_ref, size, MODE_SLICES, MODE_SLICES)
    factor = scale * (1.0 / 16384.0)
    across = to_row(scale)
    gram_ref[...] = (high * factor * across - jnp.where(eye_mask(size), share, 0.0)) + low * factor * across


def cyclic(size):
    rows, lanes = iota((size, size), 0), iota((size, size), 1)
    return (lanes == rows + 1) | ((rows == size - 1) & (lanes == 0))


def columns_kernel(
    ids_ref, archive_ref, parts, scale_ref, gram_ref, columns_ref, packed_ref, slices
):
    count = ids_ref.shape[0]
    total, lanes = archive_ref.shape
    modes = scale_ref.shape[0]
    starts = range(0, lanes, CHUNK)
    picker = jnp.where(ids_ref[...] == iota((count, total), 1), 1.0, 0.0).astype(BF16)
    bound = jnp.zeros((count, 1), F32)
    for start in range(0, lanes, PIECE):
        block = jnp.dot(picker, archive_ref[:, start : start + PIECE], preferred_element_type=F32)
        columns_ref[:, start : start + PIECE] = block.astype(BF16)
        bound = jnp.maximum(bound, jnp.max(jnp.abs(block), axis=1, keepdims=True))
    scale, inverse = power_of_two(bound)
    for start in range(0, lanes, PIECE):
        block = columns_ref[:, start : start + PIECE].astype(F32)
        for index, part in enumerate(slices_of(block, None, inverse, COLUMN_SLICES)):
            slices[index * count : (index + 1) * count, start : start + PIECE] = part.astype(BF16)

    whole, lead_p, lead_c = None, [], []
    height = MODE_SLICES * modes
    for start in starts:
        right = slices[:, start : start + CHUNK]
        product = dot_nt(jnp.concatenate([parts[:, start : start + CHUNK], right], axis=0), right)
        lead_p.append(product[0:modes, 0:count])
        lead_c.append(product[height : height + count, 0:count])
        whole = product if whole is None else whole + product
    by_slice = [whole[:, j * count : (j + 1) * count] for j in range(COLUMN_SLICES)]
    last = MODE_SLICES + COLUMN_SLICES - 2
    p_high, p_low = combine(lead_p, levels_of([part[0:height] for part in by_slice], modes, last)[1:])
    last = 2 * COLUMN_SLICES - 1
    c_high, c_low = combine(lead_c, levels_of([part[height:] for part in by_slice], count, last)[1:])
    across = to_row(scale)
    factor = scale_ref[...] * (1.0 / 16384.0)
    p_high, p_low = p_high * factor * across, p_low * factor * across
    factor = scale * (1.0 / 16384.0)
    c_high, c_low = c_high * factor * across, c_low * factor * across
    n = count
    gram = gram_ref[...]
    last_block = gram[n:, n:]
    last_diagonal = jnp.sum(jnp.where(eye_mask(n), last_block, 0.0), axis=1, keepdims=True)
    c_low = jnp.where(cyclic(n), last_diagonal, c_low)
    corner = jnp.where(iota((n, n), 0) >= iota((n, n), 1), gram[0:n, 0:n], last_block)
    top = jnp.concatenate([p_high[0:n], p_low[0:n], p_high[n:], p_low[n:]], axis=1)
    low = jnp.concatenate([c_high, c_low, gram[n:, 0:n], corner], axis=1)
    for index in range(packed_ref.shape[0]):
        packed_ref[index, 0:n, :] = top
        packed_ref[index, n:, :] = low


def sum_pairs(load, count, place, n):
    high = load(0)
    error = jnp.zeros_like(high)
    for index in range(1, count):
        high, part = two_sum(high, load(index))
        error = error + part
    rows, lanes = iota(high.shape, 0), iota(high.shape, 1)
    top_takes = (lanes // n) % 2 == 1
    lane = lanes - n
    special = (lane == rows + 1) | ((rows == n - 1) & (lane == 0))
    low_takes = (lane >= 0) & (lane < n) & jnp.logical_not(special)
    takes = jnp.where(place == 0, jnp.where(top_takes, 1.0, 0.0), jnp.where(low_takes, 1.0, 0.0))
    return high + takes * pltpu.roll(error, n, 1)


def half_kernel(place_ref, both_ref, out_ref):
    copies, rows, _ = out_ref.shape
    start = pl.multiple_of(place_ref[0] * rows, 8)
    total = sum_pairs(lambda index: both_ref[index, pl.ds(start, rows), :], both_ref.shape[0], place_ref[0], rows)
    for index in range(copies):
        out_ref[index] = total


def sum_kernel(place_ref, parts_ref, out_ref):
    rows = parts_ref.shape[1]
    total = sum_pairs(lambda index: parts_ref[index], parts_ref.shape[0], place_ref[0], rows)
    for index in range(out_ref.shape[0]):
        out_ref[index] = total


def high_dot(a, b):
    return jnp.dot(a, b, precision=HIGH, preferred_element_type=F32)


def widen(a):
    return jnp.concatenate([a, jnp.zeros((a.shape[0], 128 - a.shape[1]), F32)], axis=1)


def pieces_of(a):
    high = a.astype(BF16)
    return high, (a - high.astype(F32)).astype(BF16)


def wide_dot(left, right):
    a_high, a_low = left
    b_high, b_low = right
    none = jnp.zeros((128 - b_high.shape[0], 128), BF16)
    down = jnp.concatenate([b_high, none, b_low, none, b_high, none], axis=0)
    return jnp.dot(jnp.concatenate([a_low, a_high, a_high], axis=1), down, preferred_element_type=F32)


def slice_product(left, right, level_count):
    size = left[0].shape[0]
    stacked = jnp.concatenate(left, axis=0).astype(BF16)
    products = []
    for j, part in enumerate(right):
        rows = (level_count - j) * size
        products.append(jnp.dot(stacked[0:rows], part.astype(BF16), preferred_element_type=F32))
    levels = levels_of(products, size, level_count)
    return combine(levels[0:1], levels[1:])


def triangle(high, low):
    size = high.shape[0]
    rows = iota((size, size), 0)
    for j in range(size - 1):
        row_high, row_low = high[j : j + 1, :], low[j : j + 1, :]
        below = iota((size, 1), 0) > j
        col_high = jnp.where(below, high[:, j : j + 1], 0.0)
        col_low = jnp.where(below, low[:, j : j + 1], 0.0)
        d_high, d_low = row_high[:, j : j + 1], row_low[:, j : j + 1]
        q_high = 1.0 / d_high
        p_high, p_low = two_product(d_high, q_high)
        q_low = q_high * (((1.0 - p_high) - p_low) - d_low * q_high)
        w_high, w_error = two_product(col_high, q_high)
        w_low = w_error + (col_high * q_low + col_low * q_high)
        u_high, u_error = two_product(w_high, row_high)
        u_low = u_error + (w_high * row_low + w_low * row_high)
        s_high, s_error = two_sum(high, -u_high)
        s_low = s_error + (low - u_low)
        high = s_high + s_low
        low = s_low - (high - s_high)
    pivots = jnp.sum(jnp.where(eye_mask(size), high, 0.0), axis=1, keepdims=True)
    return jnp.where(iota((size, size), 1) >= rows, high * lax.rsqrt(pivots), 0.0)


def dense(packed, values, total_rows):
    n = packed.shape[0] // 2
    m = 2 * n
    width = m + n
    square_scale = 1.0 / total_rows
    scale = math.sqrt(square_scale)

    def block(row, lane):
        return packed[row * n : (row + 1) * n, lane * n : (lane + 1) * n]

    p_high = jnp.concatenate([block(0, 0), block(0, 2)], axis=0)
    p_low = jnp.concatenate([block(0, 1), block(0, 3)], axis=0)
    p_high, p_low = two_sum(p_high, p_low)
    stored, corner, side = block(1, 1), block(1, 3), block(1, 2)
    special = cyclic(n)
    last_diagonal = jnp.sum(jnp.where(special, stored, 0.0), axis=1, keepdims=True)
    c_high, c_low = two_sum(block(1, 0), jnp.where(special, stored.T, stored))
    rows, lanes = iota((n, n), 0), iota((n, n), 1)
    turned_corner = corner.T
    first_block = jnp.where(rows >= lanes, corner, turned_corner)
    last_block = jnp.where(rows > lanes, turned_corner, jnp.where(rows < lanes, corner, last_diagonal))
    excess = jnp.concatenate(
        [jnp.concatenate([first_block, side.T], axis=1), jnp.concatenate([side, last_block], axis=1)], axis=0
    )
    eye_m = jnp.where(eye_mask(m), 1.0, 0.0)
    t_high, t_low = two_sum(eye_m, -excess)

    t_scale, t_inverse = power_of_two(jnp.max(jnp.max(jnp.abs(t_high), axis=1, keepdims=True), axis=0, keepdims=True))
    p_scale, p_inverse = power_of_two(jnp.max(jnp.abs(p_high), axis=0, keepdims=True))
    p_slices = slices_of(p_high, p_low, p_inverse, DENSE_SLICES)
    h_high, h_low = slice_product(slices_of(t_high, t_low, t_inverse, DENSE_SLICES), p_slices, DENSE_SLICES)
    h_scale, h_inverse = power_of_two(jnp.max(jnp.abs(h_high), axis=0, keepdims=True))
    pt_slices = [part.T for part in p_slices]
    q_high, q_low = slice_product(pt_slices, slices_of(h_high, h_low, h_inverse, DENSE_SLICES), DENSE_SLICES)
    factor = to_column(p_scale) * (1.0 / 16384.0)
    across = h_scale * (p_scale * (t_scale * (1.0 / 16384.0)))
    q_high, q_low = q_high * factor * across, q_low * factor * across
    r_high, r_error = two_sum(c_high, -q_high)
    one_high, one_low = two_sum(r_high, r_error + (c_low - q_low))

    eye_n = eye_mask(n)
    own = jnp.sum(jnp.where(eye_n, one_high, 0.0), axis=0, keepdims=True)
    energy = jnp.sum(jnp.where(eye_n, c_high, 0.0), axis=0, keepdims=True)
    novelty = own / energy

    values_column = to_column(values)
    projection = p_high * scale
    turned = projection.T
    mixed = projection * values_column
    kernel_top = jnp.concatenate([eye_m * (values_column * values_column), mixed], axis=1)
    gram = one_high * square_scale
    kernel_low = jnp.concatenate([mixed.T, high_dot(turned, projection) + gram], axis=1)
    inner = jnp.concatenate([kernel_top, kernel_low], axis=0)
    eye_w = jnp.where(eye_mask(width), 1.0, 0.0)
    total = jnp.sum(jnp.sum(inner * eye_w, axis=1, keepdims=True), axis=0, keepdims=True)
    shifted = widen((inner - (total / width) * eye_w) / total)
    slope = eye = widen(eye_w)
    origin = -1.0 / width
    for _ in range(NEWTON):
        pieces = pieces_of(shifted)
        squared = wide_dot(pieces, pieces)
        divided = (origin * origin) * eye + origin * shifted + squared
        slope = 1.5 * slope - 0.5 * wide_dot(pieces_of(slope), pieces_of(divided))
        shifted = 1.5 * shifted - 0.5 * wide_dot(pieces, pieces_of(squared))
        origin = 1.5 * origin - 0.5 * origin * origin * origin
    blend = 0.5 * (eye_w + shifted[:, 0:width])
    slope = slope[:, 0:width] * (0.5 / total)

    upper = triangle(one_high, one_low) * scale
    core = jnp.concatenate(
        [
            jnp.concatenate([eye_m * values_column, projection], axis=1),
            jnp.concatenate([jnp.zeros((n, m), F32), upper], axis=1),
        ],
        axis=0,
    )
    half = high_dot(core, slope)
    projector = (0.5 * (1.0 + origin)) * eye_w + lax.dot_general(
        half, core, (((1,), (1,)), ((), ())), precision=HIGH, preferred_element_type=F32
    )
    weights = jnp.concatenate([blend[:, 0:m] * (values * math.sqrt(total_rows)), blend[:, m:]], axis=1)
    return weights, projector, novelty


def finish_kernel(
    total_rows,
    packed_ref,
    values_ref,
    pair,
    columns,
    filtered_hbm,
    projector_ref,
    novelty_ref,
    filtered,
    left_sem,
):
    modes = values_ref.shape[1]
    lanes = pair.shape[1]
    senders, rows = packed_ref.shape[0] // 2, packed_ref.shape[1]
    top = sum_pairs(lambda index: packed_ref[2 * index], senders, 0, rows)
    low = sum_pairs(lambda index: packed_ref[2 * index + 1], senders, 1, rows)
    weights, projector, novelty = dense(jnp.concatenate([top, low], axis=0), values_ref[...], total_rows)
    rounded = weights.astype(BF16)
    rest = (weights - rounded.astype(F32)).astype(BF16)
    left = jnp.concatenate(
        [rounded[:, 0:modes], rounded[:, 0:modes], rest[:, 0:modes], rounded[:, modes:], rest[:, modes:]], axis=1
    )
    stores = []
    for start in range(0, lanes, PIECE):
        where = slice(start, start + PIECE)
        first, second, third = pair[0:modes, where], pair[modes:, where], columns[:, where]
        right = jnp.concatenate([first, second, first, third, third], axis=0)
        filtered[:, where] = jnp.dot(left, right, preferred_element_type=F32)
        store = pltpu.make_async_copy(
            filtered.at[:, pl.ds(start, PIECE)], filtered_hbm.at[:, pl.ds(start, PIECE)], left_sem.at[len(stores)]
        )
        store.start()
        stores.append(store)
    projector_ref[...] = projector
    novelty_ref[...] = novelty
    for store in stores:
        store.wait()


def vmem(count):
    return [pl.BlockSpec(memory_space=pltpu.VMEM)] * count


def shape(dims, dtype=F32):
    return jax.ShapeDtypeStruct(dims, dtype)


def kept(dims, dtype=F32):
    return shape(dims, dtype) if INTERPRET else pltpu.VMEM(dims, dtype)


def params():
    return pltpu.CompilerParams(vmem_limit_bytes=24 * 1024 * 1024)


def prepare(basis, share):
    modes, lanes = basis.shape
    return pl.pallas_call(
        functools.partial(modes_kernel, share),
        out_shape=(
            kept((MODE_SLICES * modes, lanes), BF16),
            kept((modes, 1)),
            kept((2 * modes, lanes), BF16),
            kept((modes, modes)),
        ),
        in_specs=vmem(1),
        out_specs=tuple(vmem(4)),
        interpret=INTERPRET,
        compiler_params=params(),
        name="modes",
    )(basis)


def gather(ids, everything, parts, scale, gram, copies):
    count, lanes = ids.shape[0], everything.shape[1]
    return pl.pallas_call(
        columns_kernel,
        out_shape=(kept((count, lanes), BF16), kept((copies, 2 * count, 128))),
        in_specs=vmem(5),
        out_specs=tuple(vmem(2)),
        scratch_shapes=[
            pltpu.VMEM((COLUMN_SLICES * count, lanes), BF16),
        ],
        interpret=INTERPRET,
        compiler_params=params(),
        name="columns",
    )(ids, everything, parts, scale, gram)


def add_up(place, parts, copies):
    return pl.pallas_call(
        sum_kernel,
        out_shape=kept((copies,) + parts.shape[1:]),
        in_specs=[pl.BlockSpec(memory_space=pltpu.SMEM)] + vmem(1),
        out_specs=vmem(1)[0],
        interpret=INTERPRET,
        compiler_params=params(),
        name="add",
    )(place, parts)


def take_half(place, both, copies):
    return pl.pallas_call(
        half_kernel,
        out_shape=kept((copies, both.shape[1] // 2, 128)),
        in_specs=[pl.BlockSpec(memory_space=pltpu.SMEM)] + vmem(1),
        out_specs=vmem(1)[0],
        interpret=INTERPRET,
        compiler_params=params(),
        name="half",
    )(place, both)


def finish(total_rows, packed, values, pair, columns):
    modes, count, lanes = values.shape[1], columns.shape[0], columns.shape[1]
    width = modes + count
    anywhere = pl.BlockSpec(memory_space=pl.ANY)
    return pl.pallas_call(
        functools.partial(finish_kernel, total_rows),
        out_shape=(shape((width, lanes)), shape((width, width)), shape((1, count))),
        in_specs=vmem(4),
        out_specs=(anywhere,) + tuple(vmem(2)),
        scratch_shapes=[
            pltpu.VMEM((width, lanes), F32),
            pltpu.SemaphoreType.DMA((lanes // PIECE,)),
        ],
        interpret=INTERPRET,
        compiler_params=params(),
        name="finish",
    )(packed, values, pair, columns)


def exchange(copies, axes):
    return near(lax.all_to_all(copies, axes, 0, 0, tiled=True))


def near(array):
    return pltpu.with_memory_space_constraint(array, pltpu.VMEM)


def per_device(basis, values, archive, window_ids):
    devices = 1
    for name in ALL:
        devices *= lax.axis_size(name)
    total_rows = basis.shape[1] * devices
    everything = near(lax.all_to_all(archive, ("x", "c"), split_axis=1, concat_axis=0, tiled=True))
    parts, scale, pair, gram = prepare(basis, 1.0 / devices)
    columns, packed = gather(near(window_ids[:, None]), everything, parts, scale, gram, 1)
    place = lax.axis_index("c").astype(jnp.int32)[None]
    both = near(lax.all_gather(packed, "c", axis=0, tiled=True))
    packed = take_half(place, both, lax.axis_size("y"))
    packed = add_up(place, exchange(packed, ("y",)), lax.axis_size("z"))
    packed = add_up(place, exchange(packed, ("z",)), lax.axis_size("x") * lax.axis_size("c"))
    packed = exchange(packed, ("x", "c"))
    filtered, projector, novelty = finish(total_rows, packed, near(values[None, :]), pair, columns)
    return (filtered, projector, novelty.reshape(-1))


def solution(mesh):
    fine = Mesh(mesh.devices.reshape(8, 8, 4, 2), ALL)
    placed = (P(None, ALL), P(), P(("x", "c"), ("y", "z")), P())
    return jax.shard_map(
        per_device,
        mesh=fine,
        in_specs=placed,
        out_specs=(P(None, ALL), P(), P()),
        check_vma=False,
    )
```
